32 devices in a mesh: row: 8 (over y, x, core), col: 4 (over z).
Axes of the slice: x: 2, y: 2, z: 4, core: 2. Of those that a mesh axis runs over, the one named last changes fastest.
Arguments:
- blocks: bfloat16 [8, 4, 320, 128, 128], P('row', 'col'), may hold values from -0.1875 to 0.1875
- block_rows: int32 [8, 4, 320], P('row', 'col'), may hold values from 0 to 1023, as said below
- block_cols: int32 [8, 4, 320], P('row', 'col'), may hold values from 0 to 1023, as said below
- counts: int32 [8, 4], P('row', 'col'), may hold values from 160 to 320, as said below
- panel: bfloat16 [32, 131072], P(None, ('row', 'col'))
Outputs:
- basis: bfloat16 [32, 131072], P(None, ('row', 'col'))
- factor: float32 [32, 32], replicated
The draws below stay inside these ranges and needn't reach their ends.
Inputs may be any that keep to these rules, and one draw needn't show every extreme that they name: `block_rows`: split the block-rows into shards of 32 in order; every block of device (r, c) lies in a block-row of a shard whose index modulo 4 is c. Pairs may repeat. `block_cols`: every block of device (r, c) lies in a block-column of a shard whose index divided by 4 is r. `counts`: some device has all 320 slots live.
All inputs are finite; a program needn't handle non-finite values.
Results may differ from the reference program's by a relative error of at most 0.001.
Values may be sent and summed in bfloat16 or wider, within the bound.
No kernel may reach another device: no remote copies, remote signals or barrier semaphores. Data moves between devices by JAX's collectives and lax.ppermute only.
A program may use at most 64 MiB of HBM per device.

```python
import math
import jax
import jax.numpy as jnp
from jax import lax

BLK = 128
PANEL = 32
NB_DEV = 32
GRID_R = 8
GRID_C = 4
SLOTS = 320
NBLK = 1024
NROWS = 131072


def local_indices(key):
    key_rows = jax.random.fold_in(key, 11)
    key_cols = jax.random.fold_in(key, 12)
    local_row = jax.random.randint(key_rows, (GRID_R, GRID_C, SLOTS), 0, GRID_R * NB_DEV)
    local_col = jax.random.randint(key_cols, (GRID_R, GRID_C, SLOTS), 0, GRID_C * NB_DEV)
    return (local_row, local_col)


def draw_block_rows(key, part):
    local_row, local_col = local_indices(key)
    col_idx = jnp.arange(GRID_C, dtype=jnp.int32)[None, :, None]
    shard = local_row // NB_DEV * GRID_C + col_idx
    return (shard * NB_DEV + local_row % NB_DEV).astype(jnp.int32)


def draw_block_cols(key, part):
    local_row, local_col = local_indices(key)
    row_idx = jnp.arange(GRID_R, dtype=jnp.int32)[:, None, None]
    return (row_idx * GRID_C * NB_DEV + local_col).astype(jnp.int32)


def draw_counts(key, part):
    key_base = jax.random.fold_in(key, 21)
    key_pick = jax.random.fold_in(key, 22)
    base = jax.random.randint(key_base, (GRID_R * GRID_C,), SLOTS // 2, SLOTS + 1)
    chosen = jax.random.randint(key_pick, (), 0, GRID_R * GRID_C)
    filled = jnp.where(jnp.arange(GRID_R * GRID_C) == chosen, SLOTS, base)
    return filled.reshape(GRID_R, GRID_C).astype(jnp.int32)


def draw_panel(key, part):
    key_base = jax.random.fold_in(key, 31)
    key_rows = jax.random.fold_in(key, 32)
    key_cols = jax.random.fold_in(key, 33)
    row_scale = jnp.exp(jax.random.uniform(key_rows, (1, NROWS), jnp.float32, 0.0, math.log(10.0)))
    col_scale = jnp.exp(jax.random.uniform(key_cols, (PANEL, 1), jnp.float32, 0.0, math.log(10.0)))
    base = jax.random.normal(key_base, (PANEL, NROWS), jnp.float32)
    return (0.3 * base * row_scale * col_scale).astype(jnp.bfloat16)


def level_of(own_key, shape, pieces, least, top_value):
    level = 1.0
    for axis_at, parts in pieces:
        draws = jax.random.uniform(jax.random.fold_in(jax.random.fold_in(own_key, 6), axis_at), (parts,), jnp.float32, least / len(pieces), top_value / len(pieces))
        level = level * jnp.repeat(jnp.exp(draws), shape[axis_at] // parts).reshape((-1,) + (1,) * (len(shape) - 1 - axis_at))
    return level


def gaussian(own_key, extent, deviation, limit, pieces=(), kind=jnp.bfloat16):
    entries = deviation * jax.random.normal(own_key, extent, jnp.float32)
    if pieces:
        entries = entries * level_of(own_key, extent, pieces, -0.22, 0.18)
    return jnp.clip(entries, -limit, limit).astype(kind)


def setup_inputs(seed: int = 0) -> dict:
    arg_keys = jax.random.split(jax.random.key(seed), 6)
    return {
        "blocks": gaussian(arg_keys[0], (GRID_R, GRID_C, SLOTS, BLK, BLK), (BLK * 8) ** -0.5, 0.1875, ((0, 8), (1, 4))),
        "block_rows": draw_block_rows(jax.random.fold_in(arg_keys[5], 71), 0),
        "block_cols": draw_block_cols(jax.random.fold_in(arg_keys[5], 71), 0),
        "counts": draw_counts(jax.random.fold_in(arg_keys[5], 71), 0),
        "panel": draw_panel(jax.random.fold_in(arg_keys[5], 71), 0),
    }


def reference(blocks, block_rows, block_cols, counts, panel):
    tiles = panel.reshape(PANEL, NBLK, BLK)
    flat_blocks = blocks.reshape(GRID_R * GRID_C, SLOTS, BLK, BLK)
    flat_rows = block_rows.reshape(GRID_R * GRID_C, SLOTS).astype(jnp.int32)
    flat_cols = block_cols.reshape(GRID_R * GRID_C, SLOTS).astype(jnp.int32)
    flat_counts = counts.reshape(GRID_R * GRID_C).astype(jnp.int32)

    def add_device(total, item):
        values, row_ids, col_ids, live_count = item
        picked = jnp.take(tiles, col_ids, axis=1).astype(jnp.float32)
        live = (jnp.arange(SLOTS, dtype=jnp.int32) < live_count).astype(jnp.float32)
        terms = jnp.einsum('psk,sjk->spj', picked, values.astype(jnp.float32), precision=lax.Precision.HIGHEST)
        terms = terms * live[:, None, None]
        return (total.at[row_ids].add(terms), None)
    start = jnp.zeros((NBLK, PANEL, BLK), jnp.float32)
    total, unused = lax.scan(add_device, start, (flat_blocks, flat_rows, flat_cols, flat_counts))
    product_t = jnp.transpose(total, (1, 0, 2)).reshape(PANEL, NROWS)
    gram = jnp.dot(product_t.astype(jnp.float32), product_t.T.astype(jnp.float32), precision=lax.Precision.HIGHEST, preferred_element_type=jnp.float32) / NROWS
    lower = jnp.linalg.cholesky(gram)
    basis = jax.scipy.linalg.solve_triangular(lower, product_t, lower=True)
    return (basis.astype(jnp.bfloat16), lower.T)
```

```python
import functools

import jax
import jax.numpy as jnp
from jax import lax
from jax.experimental import pallas as pl
from jax.experimental.pallas import tpu as pltpu
from jax.sharding import PartitionSpec as P

GROUP = 32


def flips(size, mask):
    return [(i, i ^ mask) for i in range(size)]


def gather_panel(panel, size):
    cols = panel.shape[1]
    if size != 4:
        held = [(0, panel)]
        bit = 1
        while bit < size:
            held = held + [(rel ^ bit, lax.ppermute(x, "col", flips(size, bit))) for rel, x in held]
            bit *= 2
        return [(rel, 0, x) for rel, x in held]
    half = cols // 2
    low, high = panel[:, :half], panel[:, half:]
    near_high = lax.ppermute(high, "col", flips(4, 1))
    far_low = lax.ppermute(low, "col", flips(4, 3))
    near_low = lax.ppermute(low, "col", flips(4, 1))
    far_high = lax.ppermute(high, "col", flips(4, 3))
    cross_high = lax.ppermute(near_high, "col", flips(4, 3))
    cross_low = lax.ppermute(far_low, "col", flips(4, 1))
    return [
        (0, 0, panel),
        (1, 0, near_low),
        (1, half, near_high),
        (3, 0, far_low),
        (3, half, far_high),
        (2, 0, cross_low),
        (2, half, cross_high),
    ]


def multiply_kernel(where, nb, n_lists, *refs):
    slots_ref, rows_ref, cols_ref, bounds_ref = refs[:n_lists]
    piece_refs = refs[n_lists : n_lists + len(where)]
    blocks_ref, acc_ref, tiles = refs[n_lists + len(where) :]
    width = blocks_ref.shape[-1]
    for (rel, first), ref in zip(where, piece_refs):
        tiles[rel, :, first : first + ref.shape[1]] = ref[...]
    tiles[tiles.shape[0] - 1] = jnp.zeros(tiles.shape[1:], tiles.dtype)
    acc_ref[...] = jnp.zeros_like(acc_ref)
    begin, end = bounds_ref[0], bounds_ref[1]
    blank = (tiles.shape[0] - 1) * nb

    def step(g, carry):
        parts, targets = [], []
        for u in range(GROUP):
            at = begin + g * GROUP + u
            tile = jnp.where(at < end, cols_ref[at], blank)
            left = tiles[tile // nb, :, pl.ds(pl.multiple_of(tile % nb * width, width), width)]
            parts.append(
                lax.dot_general(
                    left, blocks_ref[slots_ref[at]], (((1,), (1,)), ((), ())), preferred_element_type=jnp.float32
                )
            )
            targets.append(rows_ref[at])
        for part, target in zip(parts, targets):
            acc_ref[target] += part
        return carry

    lax.fori_loop(0, (end - begin + GROUP - 1) // GROUP, step, 0)


def multiply(lists, pieces, blocks, rows, n_shards, nb):
    where = [(rel, first) for rel, first, _ in pieces]
    panel_cols, shard_cols = pieces[0][2].shape
    vmem = pl.BlockSpec(memory_space=pltpu.VMEM)
    smem = pl.BlockSpec(memory_space=pltpu.SMEM)
    width = blocks.shape[-1]
    slots = blocks.shape[0]
    return pl.pallas_call(
        functools.partial(multiply_kernel, where, nb, len(lists)),
        out_shape=jax.ShapeDtypeStruct((rows, panel_cols, width), jnp.float32),
        in_specs=[smem] * len(lists) + [vmem] * (len(pieces) + 1),
        out_specs=vmem,
        scratch_shapes=[pltpu.VMEM((n_shards + 1, panel_cols, shard_cols), pieces[0][2].dtype)],
        compiler_params=pltpu.CompilerParams(vmem_limit_bytes=36 << 20),
        cost_estimate=pl.CostEstimate(
            flops=slots * panel_cols * width * width, bytes_accessed=slots * width * width, transcendentals=0
        ),
        name="multiply",
    )(*lists, *[x for _, _, x in pieces], blocks)


def split_kernel(a_ref, b_ref, *outs):
    at = 0
    for out in outs:
        n = out.shape[0]
        out[...] = a_ref[at : at + n] + b_ref[at : at + n]
        at += n


def add_and_split(a, b, parts):
    n = a.shape[0] // parts
    vmem = pl.BlockSpec(memory_space=pltpu.VMEM)
    return pl.pallas_call(
        split_kernel,
        out_shape=[jax.ShapeDtypeStruct((n,) + a.shape[1:], a.dtype)] * parts,
        in_specs=[vmem, vmem],
        out_specs=[vmem] * parts,
        compiler_params=pltpu.CompilerParams(vmem_limit_bytes=36 << 20),
        name="add_and_split",
    )(a, b)


def gram_kernel(*refs):
    ins, (rows_ref, gram_ref) = refs[:-2], refs[-2:]
    s = rows_ref.shape[1]
    total = jnp.zeros((s, s), jnp.float32)
    at = 0
    for a, b in zip(ins[0::2], ins[1::2]):
        for i in range(a.shape[0]):
            row = a[i] + b[i]
            rows_ref[at] = row
            total += lax.dot_general(
                row, row, (((1,), (1,)), ((), ())), precision=lax.Precision.HIGHEST, preferred_element_type=jnp.float32
            )
            at += 1
    gram_ref[...] = jnp.broadcast_to(total[None], gram_ref.shape)


def gram_of(pairs, copies):
    vmem = pl.BlockSpec(memory_space=pltpu.VMEM)
    flat = [x for pair in pairs for x in pair]
    _, s, width = flat[0].shape
    rows = sum(a.shape[0] for a, _ in pairs)
    return pl.pallas_call(
        gram_kernel,
        out_shape=(
            jax.ShapeDtypeStruct((rows, s, width), jnp.float32),
            jax.ShapeDtypeStruct((copies, s, s), jnp.float32),
        ),
        in_specs=[vmem] * len(flat),
        out_specs=[vmem, vmem],
        name="gram",
    )(*flat)


def factor_kernel(total_rows, grams_ref, rows_ref, basis_ref, factor_ref):
    left = jnp.sum(grams_ref[...], axis=0) / total_rows
    n = left.shape[0]
    width = rows_ref.shape[2]
    ri = lax.broadcasted_iota(jnp.int32, (n, n), 0)
    ci = lax.broadcasted_iota(jnp.int32, (n, n), 1)
    inverse = jnp.where(ri == ci, 1.0, 0.0).astype(jnp.float32)
    upper = jnp.zeros((n, n), jnp.float32)
    for j in range(n):
        scale = lax.rsqrt(left[j : j + 1, j : j + 1])
        row = left[j : j + 1, :] * scale
        done = inverse[j : j + 1, :] * scale
        column = jnp.where(ri[:, j : j + 1] > j, left[:, j : j + 1] * scale, 0.0)
        left = left - column * row
        inverse = jnp.where(ri == j, done, inverse - column * done)
        upper = jnp.where(ri == j, jnp.where(ci >= j, row, 0.0), upper)
    factor_ref[...] = upper
    for i in range(rows_ref.shape[0]):
        basis_ref[:, i * width : (i + 1) * width] = jnp.dot(
            inverse, rows_ref[i], precision=lax.Precision.HIGHEST, preferred_element_type=jnp.float32
        ).astype(basis_ref.dtype)


def finish(grams, rows, total_rows):
    vmem = pl.BlockSpec(memory_space=pltpu.VMEM)
    n, s, width = rows.shape
    return pl.pallas_call(
        functools.partial(factor_kernel, total_rows),
        out_shape=(
            jax.ShapeDtypeStruct((s, n * width), jnp.bfloat16),
            jax.ShapeDtypeStruct((s, s), jnp.float32),
        ),
        in_specs=[vmem, vmem],
        out_specs=[vmem, vmem],
        name="finish",
    )(grams, rows)


def on_device(blocks, block_rows, block_cols, counts, panel):
    width = blocks.shape[-1]
    slots = blocks.shape[2]
    nb = panel.shape[1] // width
    grid_rows = lax.axis_size("row")
    grid_cols = lax.axis_size("col")
    span = nb * grid_cols
    bits = grid_rows.bit_length() - 1
    me_row, me_col = lax.axis_index("row"), lax.axis_index("col")

    global_rows, global_cols = block_rows[0, 0], block_cols[0, 0]
    owner = (global_rows // span) ^ me_row
    inner = global_rows % nb
    half = nb // 2
    rest = owner >> 1
    mirrored = jnp.zeros_like(rest)
    for b in range(bits - 1):
        mirrored = mirrored | (((rest >> b) & 1) << (bits - 2 - b))
    second = inner >= half
    target = jnp.where(second, rest + grid_rows // 2, mirrored) * half + jnp.where(second, inner - half, inner)
    local_cols = global_cols % span
    tile = ((local_cols // nb) ^ me_col) * nb + local_cols % nb

    live = jnp.arange(slots, dtype=jnp.int32) < counts[0, 0]
    key = jnp.where(live, jnp.where(owner & 1 == 1, 0, 1), 2)
    order_key = key * slots + jnp.arange(slots, dtype=jnp.int32)
    rank = jnp.sum((order_key[None, :] < order_key[:, None]).astype(jnp.int32), axis=1)
    place = jnp.arange(slots + GROUP, dtype=jnp.int32)
    hit = (rank[None, :] == place[:, None]).astype(jnp.int32)
    pack = (jnp.arange(slots, dtype=jnp.int32) * (grid_rows * nb) + target) * span + tile
    packed = jnp.sum(hit * pack[None, :], axis=1)
    cols_list = packed % span
    rows_list = packed // span % (grid_rows * nb)
    slots_list = packed // span // (grid_rows * nb)
    sent = jnp.sum((key == 0).astype(jnp.int32))
    alive = jnp.sum(live.astype(jnp.int32))

    pieces = gather_panel(panel, grid_cols)
    args = (pieces, blocks[0, 0], grid_rows * nb // 2, grid_cols, nb)
    send = multiply((slots_list, rows_list, cols_list, jnp.stack([jnp.zeros_like(sent), sent])), *args)
    got = lax.ppermute(send, "row", flips(grid_rows, 1))
    keep = multiply((slots_list, rows_list, cols_list, jnp.stack([sent, alive])), *args)

    keep_a, send_a, keep_b, send_b = add_and_split(keep, got, 4)
    for stage in range(1, bits):
        got_a = lax.ppermute(send_a, "row", flips(grid_rows, 1 << stage))
        got_b = lax.ppermute(send_b, "row", flips(grid_rows, 1 << (bits - stage)))
        if stage < bits - 1:
            keep_a, send_a = add_and_split(keep_a, got_a, 2)
            keep_b, send_b = add_and_split(keep_b, got_b, 2)

    devices = grid_rows * grid_cols
    rows, grams = gram_of([(keep_a, got_a), (keep_b, got_b)], devices)
    s = grams.shape[1]
    grams = lax.all_to_all(grams.reshape(devices, s * s // width, width), ("row", "col"), 0, 0, tiled=True)
    return finish(grams.reshape(devices, s, s), rows, nb * width * devices)


def solution(mesh):
    in_specs = (
        P("row", "col", None, None, None),
        P("row", "col", None),
        P("row", "col", None),
        P("row", "col"),
        P(None, ("row", "col")),
    )
    out_specs = (P(None, ("row", "col")), P())
    return jax.shard_map(
        on_device, mesh=mesh, in_specs=in_specs, out_specs=out_specs, check_vma=False
    )
```

```python
import functools

import jax
import jax.numpy as jnp
from jax import lax
from jax.experimental import pallas as pl
from jax.experimental.pallas import tpu as pltpu
from jax.sharding import PartitionSpec as P

GROUP = 32
VMEM_LIMIT = 16 << 20


def flips(size, mask):
    return [(i, i ^ mask) for i in range(size)]


def gather_panel(panel, size, after):
    cols = panel.shape[1]
    if size != 4:
        held = [(0, panel)]
        bit = 1
        while bit < size:
            held = held + [(rel ^ bit, lax.ppermute(x, "col", flips(size, bit))) for rel, x in held]
            bit *= 2
        return [[(0, 0, panel)], [(rel, 0, x) for rel, x in held[1:]]], after
    half = cols // 2
    low, high = panel[:, :half], panel[:, half:]
    near_high = lax.ppermute(high, "col", flips(4, 1))
    far_low = lax.ppermute(low, "col", flips(4, 3))
    near_low = lax.ppermute(low, "col", flips(4, 1))
    far_high = lax.ppermute(high, "col", flips(4, 3))
    near_high, far_low, after = lax.optimization_barrier((near_high, far_low, after))
    cross_high = lax.ppermute(near_high, "col", flips(4, 3))
    cross_low = lax.ppermute(far_low, "col", flips(4, 1))
    return [
        [(0, 0, low), (0, half, high)],
        [(1, 0, near_low), (1, half, near_high), (3, 0, far_low), (3, half, far_high)],
        [(2, 0, cross_low), (2, half, cross_high)],
    ], after


def multiply_kernel(where, nb, bucket, origin, *refs):
    slots_ref, rows_ref, cols_ref, bounds_ref = refs[:4]
    piece_refs = refs[4 : 4 + len(where)]
    blocks_ref = refs[4 + len(where)]
    acc_ref, tiles = refs[-2:]
    width = blocks_ref.shape[-1]
    for (shard, first), ref in zip(where, piece_refs):
        tiles[shard, :, first : first + ref.shape[1]] = ref[...]
    tiles[tiles.shape[0] - 1] = jnp.zeros(tiles.shape[1:], tiles.dtype)
    if origin is None:
        acc_ref[...] = jnp.zeros_like(acc_ref)
    elif origin >= 0:
        acc_ref[...] = refs[-3][origin : origin + acc_ref.shape[0]]
    begin, end = bounds_ref[bucket], bounds_ref[bucket + 1]
    blank = (tiles.shape[0] - 1) * nb

    def step(g, carry):
        parts, targets = [], []
        for u in range(GROUP):
            at = begin + g * GROUP + u
            tile = jnp.where(at < end, cols_ref[at], blank)
            left = tiles[tile // nb, :, pl.ds(pl.multiple_of(tile % nb * width, width), width)]
            parts.append(
                lax.dot_general(
                    left, blocks_ref[slots_ref[at]], (((1,), (1,)), ((), ())), preferred_element_type=jnp.float32
                )
            )
            row = rows_ref[at] - max(origin or 0, 0)
            targets.append(jnp.clip(row, 0, acc_ref.shape[0] - 1) if origin is not None and origin >= 0 else row)
        for part, target in zip(parts, targets):
            acc_ref[target] += part
        return carry

    lax.fori_loop(0, (end - begin + GROUP - 1) // GROUP, step, 0)


def multiply(lists, bucket, pieces, blocks, nb, rows, total=None, origin=None):
    shards = sorted({rel for rel, _, _ in pieces})
    where = [(shards.index(rel), first) for rel, first, _ in pieces]
    panel_cols = pieces[0][2].shape[0]
    vmem = pl.BlockSpec(memory_space=pltpu.VMEM)
    smem = pl.BlockSpec(memory_space=pltpu.SMEM)
    slots, width, _ = blocks.shape
    operands = [*lists, *[x for _, _, x in pieces], blocks] + ([] if total is None else [total])
    if total is None:
        origin = None
    share = slots * len(pieces) // 8
    return pl.pallas_call(
        functools.partial(multiply_kernel, where, nb, bucket, origin),
        out_shape=jax.ShapeDtypeStruct((rows, panel_cols, width), jnp.float32),
        in_specs=[smem] * 4 + [vmem] * (len(operands) - 4),
        out_specs=vmem,
        scratch_shapes=[pltpu.VMEM((len(shards) + 1, panel_cols, nb * width), pieces[0][2].dtype)],
        input_output_aliases={len(operands) - 1: 0} if origin == -1 else {},
        compiler_params=pltpu.CompilerParams(vmem_limit_bytes=VMEM_LIMIT),
        cost_estimate=pl.CostEstimate(
            flops=share * panel_cols * width * width * 2, bytes_accessed=share * width * width * 2, transcendentals=0
        ),
        name="multiply",
    )(*operands)


def encode(rows, out_ref):
    shape = rows[0].shape
    lane = lax.broadcasted_iota(jnp.int32, shape, 1)
    scales = jnp.zeros(shape, jnp.int32)
    for i, row in enumerate(rows):
        top = jnp.max(jnp.abs(row), axis=1, keepdims=True)
        code = jnp.ceil(jnp.log2(jnp.maximum(top, 2.0**-100)) * 128.0) + 1.0
        out_ref[i] = jnp.round(row * jnp.exp2(15.0 - code / 128.0)).astype(jnp.int32).astype(jnp.int16)
        scales = jnp.where(lane == i, jnp.broadcast_to(code.astype(jnp.int32), shape), scales)
    out_ref[len(rows)] = scales.astype(jnp.int16)


def decode(ref):
    n, shape = ref.shape[0] - 1, ref.shape[1:]
    steps = jnp.exp2(ref[n].astype(jnp.int32).astype(jnp.float32) / 128.0 - 15.0)
    return lambda i: ref[i].astype(jnp.int32).astype(jnp.float32) * jnp.broadcast_to(steps[:, i : i + 1], shape)


def reader(ref):
    return decode(ref) if ref.dtype == jnp.int16 else lambda i: ref[i]


def split_kernel(a_ref, b_ref, *outs):
    got = reader(b_ref)
    at = 0
    for keep_ref, send_ref in zip(outs[0::2], outs[1::2]):
        n = keep_ref.shape[0]
        for i in range(n):
            keep_ref[i] = a_ref[at + i] + got(at + i)
        encode([a_ref[at + n + i] + got(at + n + i) for i in range(n)], send_ref)
        at += 2 * n


def add_and_split(a, b, pairs):
    n, rest = a.shape[0] // (2 * pairs), a.shape[1:]
    vmem = pl.BlockSpec(memory_space=pltpu.VMEM)
    return pl.pallas_call(
        split_kernel,
        out_shape=[jax.ShapeDtypeStruct((n,) + rest, a.dtype), jax.ShapeDtypeStruct((n + 1,) + rest, jnp.int16)] * pairs,
        in_specs=[vmem, vmem],
        out_specs=[vmem] * (2 * pairs),
        compiler_params=pltpu.CompilerParams(vmem_limit_bytes=VMEM_LIMIT),
        name="add_and_split",
    )(a, b)


def load_kernel(blocks_ref, out_ref, sem):
    copy = pltpu.make_async_copy(blocks_ref, out_ref, sem)
    copy.start()
    copy.wait()


def load(blocks):
    return pl.pallas_call(
        load_kernel,
        out_shape=jax.ShapeDtypeStruct(blocks.shape, blocks.dtype),
        in_specs=[pl.BlockSpec(memory_space=pltpu.HBM)],
        out_specs=pl.BlockSpec(memory_space=pltpu.VMEM),
        scratch_shapes=[pltpu.SemaphoreType.DMA],
        compiler_params=pltpu.CompilerParams(vmem_limit_bytes=VMEM_LIMIT),
        cost_estimate=pl.CostEstimate(flops=0, bytes_accessed=2 * blocks.size, transcendentals=0),
        name="load",
    )(blocks)


def split3(x):
    high = x.astype(jnp.bfloat16)
    rest = x - high.astype(jnp.float32)
    middle = rest.astype(jnp.bfloat16)
    return high, middle, (rest - middle.astype(jnp.float32)).astype(jnp.bfloat16)


def gram_kernel(*refs):
    ins, (stack_ref, gram_ref) = refs[:-2], refs[-2:]
    s = ins[0].shape[1]
    products = jnp.zeros((3 * s, 3 * s), jnp.float32)
    pieces = [(a, reader(b), i) for a, b in zip(ins[0::2], ins[1::2]) for i in range(a.shape[0])]
    for at in range(0, len(pieces), 2):
        stacks = []
        for k in (0, 1):
            a, b, i = pieces[at + k]
            stack = jnp.concatenate(split3(a[i] + b(i)), axis=0)
            stack_ref[at + k] = stack
            stacks.append(stack)
        both = jnp.concatenate(stacks, axis=1)
        products += lax.dot_general(both, both, (((1,), (1,)), ((), ())), preferred_element_type=jnp.float32)
    gram = jnp.zeros((s, s), jnp.float32)
    for i in range(3):
        for j in range(3 - i):
            gram += products[i * s : (i + 1) * s, j * s : (j + 1) * s]
    height = gram_ref.shape[1]
    packed = jnp.concatenate([gram[i : i + height] for i in range(0, s, height)], axis=1)
    for i in range(gram_ref.shape[0]):
        gram_ref[i] = packed


def gram_of(pairs, copies):
    vmem = pl.BlockSpec(memory_space=pltpu.VMEM)
    flat = [x for pair in pairs for x in pair]
    _, s, width = flat[0].shape
    rows = sum(a.shape[0] for a, _ in pairs)
    return pl.pallas_call(
        gram_kernel,
        out_shape=(
            jax.ShapeDtypeStruct((rows, 3 * s, width), jnp.bfloat16),
            jax.ShapeDtypeStruct((copies, s * s // width, width), jnp.float32),
        ),
        in_specs=[vmem] * len(flat),
        out_specs=[vmem, vmem],
        compiler_params=pltpu.CompilerParams(vmem_limit_bytes=VMEM_LIMIT),
        name="gram",
    )(*flat)


def factor_kernel(total_rows, grams_ref, stack_ref, basis_ref, factor_ref):
    s = factor_ref.shape[0]
    width = grams_ref.shape[2]
    packed = jnp.sum(grams_ref[...], axis=0) / total_rows
    gram = jnp.concatenate([packed[:, i : i + s] for i in range(0, width, s)], axis=0)
    ri = lax.broadcasted_iota(jnp.int32, (s, width), 0)
    ci = lax.broadcasted_iota(jnp.int32, (s, width), 1)
    unit = jnp.where(ri == ci, 1.0, 0.0).astype(jnp.float32)[:, :s]
    work = jnp.concatenate([gram, unit, jnp.zeros((s, width - 2 * s), jnp.float32)], axis=1)
    pivots = jnp.ones((s, width), jnp.float32)
    spread = lambda x: jnp.broadcast_to(x, (s, width))
    for j in range(0, s, 2):
        k = j + 1
        first, cross, second = spread(work[j:k, j:k]), spread(work[k : k + 1, j:k]), spread(work[k : k + 1, k : k + 1])
        row1, row2 = spread(work[j:k, :]), spread(work[k : k + 1, :])
        col1, col2 = spread(work[:, j:k]), spread(work[:, k : k + 1])
        ratio = cross / first
        second = second - cross * ratio
        row2 = row2 - ratio * row1
        col2 = col2 - ratio * col1
        reduced = work - col1 * (row1 / first) - col2 * (row2 / second)
        work = jnp.where(ri > k, reduced, jnp.where(ri == k, row2, work))
        pivots = jnp.where(ri == j, first, jnp.where(ri == k, second, pivots))
    work = work * lax.rsqrt(pivots)
    factor_ref[...] = jnp.where(ci >= ri, work, 0.0)[:, :s]
    high, middle, low = split3(work[:, s : 2 * s])
    left = jnp.concatenate([high, high, high, middle, middle, low], axis=1)
    for i in range(0, stack_ref.shape[0], 2):
        both = jnp.concatenate([stack_ref[i], stack_ref[i + 1]], axis=1)
        right = jnp.concatenate([both, both[: 2 * s], both[:s]], axis=0)
        basis_ref[:, i * width : (i + 2) * width] = jnp.dot(
            left, right, preferred_element_type=jnp.float32
        ).astype(basis_ref.dtype)


def finish(grams, stack, total_rows):
    vmem = pl.BlockSpec(memory_space=pltpu.VMEM)
    n, rows3, width = stack.shape
    s = rows3 // 3
    return pl.pallas_call(
        functools.partial(factor_kernel, total_rows),
        out_shape=(
            jax.ShapeDtypeStruct((s, n * width), jnp.bfloat16),
            jax.ShapeDtypeStruct((s, s), jnp.float32),
        ),
        in_specs=[vmem, vmem],
        out_specs=[vmem, vmem],
        compiler_params=pltpu.CompilerParams(vmem_limit_bytes=VMEM_LIMIT),
        name="finish",
    )(grams, stack)


def on_device(blocks, block_rows, block_cols, counts, panel):
    width = blocks.shape[-1]
    slots = blocks.shape[2]
    nb = panel.shape[1] // width
    grid_rows = lax.axis_size("row")
    grid_cols = lax.axis_size("col")
    span = nb * grid_cols
    bits = grid_rows.bit_length() - 1
    me_row, me_col = lax.axis_index("row"), lax.axis_index("col")

    global_rows, global_cols = block_rows[0], block_cols[0]
    owner = (global_rows // span) ^ me_row
    inner = global_rows % nb
    half = nb // 2
    rest = owner >> 1
    mirrored = jnp.zeros_like(rest)
    for b in range(bits - 1):
        mirrored = mirrored | (((rest >> b) & 1) << (bits - 2 - b))
    second = inner >= half
    target = jnp.where(second, rest + grid_rows // 2, mirrored) * half + jnp.where(second, inner - half, inner)
    target = target + (owner & 1) * (grid_rows * nb // 2)
    pieces, store = gather_panel(panel, grid_cols, load(blocks[0, 0]))
    n_phases = len(pieces)
    rel_col = (global_cols % span // nb) ^ me_col
    phase, tile = jnp.zeros_like(rel_col), global_cols % nb
    for p, phase_pieces in enumerate(pieces):
        for i, rel in enumerate(sorted({rel for rel, _, _ in phase_pieces})):
            phase = jnp.where(rel_col == rel, p, phase)
            tile = jnp.where(rel_col == rel, tile + i * nb, tile)

    slot = lax.broadcasted_iota(jnp.int32, (1, slots), 1)
    key = jnp.where((phase == n_phases - 1) & (owner & 1 == 0), n_phases, phase)
    key = jnp.where(slot < counts, key, n_phases + 1)
    order_key = key * slots + slot
    rank = jnp.sum((order_key < order_key.reshape(slots, 1)).astype(jnp.int32), axis=1)
    place = lax.broadcasted_iota(jnp.int32, (slots + GROUP, slots), 0)
    pack = (slot * (grid_rows * nb) + target) * span + tile
    packed = jnp.sum(jnp.where(rank[None, :] == place, pack, 0), axis=1)
    bounds = jnp.sum((key < lax.broadcasted_iota(jnp.int32, (n_phases + 2, slots), 0)).astype(jnp.int32), axis=1)
    lists = (packed // span // (grid_rows * nb), packed // span % (grid_rows * nb), packed % span, bounds)

    kept = grid_rows * nb // 2
    total = multiply(lists, 0, pieces[0], store, nb, 2 * kept)
    for p in range(1, n_phases - 1):
        total = multiply(lists, p, pieces[p], store, nb, 2 * kept, total, -1)
    send = multiply(lists, n_phases - 1, pieces[-1], store, nb, kept, total, kept)
    got = lax.ppermute(send, "row", flips(grid_rows, 1))
    keep = multiply(lists, n_phases, pieces[-1], store, nb, kept, total, 0)

    keep_a, send_a, keep_b, send_b = add_and_split(keep, got, 2)
    for stage in range(1, bits):
        got_a = lax.ppermute(send_a, "row", flips(grid_rows, 1 << stage))
        got_b = lax.ppermute(send_b, "row", flips(grid_rows, 1 << (bits - stage)))
        if stage < bits - 1:
            keep_a, send_a = add_and_split(keep_a, got_a, 1)
            keep_b, send_b = add_and_split(keep_b, got_b, 1)

    devices = grid_rows * grid_cols
    stack, grams = gram_of([(keep_a, got_a), (keep_b, got_b)], devices)
    grams = lax.all_to_all(grams, ("row", "col"), 0, 0, tiled=True)
    return finish(grams, stack, nb * width * devices)


def solution(mesh):
    in_specs = (
        P("row", "col", None, None, None),
        P("row", "col", None),
        P("row", "col", None),
        P("row", "col"),
        P(None, ("row", "col")),
    )
    out_specs = (P(None, ("row", "col")), P())
    return jax.shard_map(
        on_device, mesh=mesh, in_specs=in_specs, out_specs=out_specs, check_vma=False
    )
```

```python
import functools

import jax
import jax.numpy as jnp
from jax import lax
from jax.experimental import pallas as pl
from jax.experimental.pallas import tpu as pltpu
from jax.sharding import PartitionSpec as P

GROUP = 32
STREAMS = 2
VMEM_LIMIT = 16 << 20
CHUNKS = 10


def flips(size, mask):
    return [(i, i ^ mask) for i in range(size)]


def near_pieces(panel, size):
    cols = panel.shape[1]
    if size != 4:
        held = [(0, panel)]
        bit = 1
        while bit < size:
            held = held + [(rel ^ bit, lax.ppermute(x, "col", flips(size, bit))) for rel, x in held]
            bit *= 2
        return [(0, 0, panel)], [(rel, 0, x) for rel, x in held[1:]]
    near = lax.ppermute(panel, "col", flips(4, 1))
    half = cols // 2
    low, high = panel[:, :half], panel[:, half:]
    far_low = lax.ppermute(low, "col", flips(4, 3))
    far_high = lax.ppermute(high, "col", flips(4, 3))
    return [(0, 0, low), (0, half, high)], [(1, 0, near), (3, 0, far_low), (3, half, far_high)]


def opposite_pieces(near, far_low):
    half = far_low.shape[1]
    cross_low = lax.ppermute(far_low, "col", flips(4, 1))
    cross_high = lax.ppermute(near[:, half:], "col", flips(4, 3))
    return [(2, 0, cross_low), (2, half, cross_high)]


def make_plan(arrival, nb, width_bits, rows_ref, cols_ref, counts_ref, plan_ref):
    slots = rows_ref.shape[-1]
    nb_bits, span_bits, row_bits = width_bits
    part = nb // STREAMS
    me_row, me_col = lax.axis_index("row"), lax.axis_index("col")
    global_rows, global_cols = rows_ref[0], cols_ref[0]
    owner = (global_rows >> span_bits) ^ me_row
    inner = global_rows & (nb - 1)
    rest = owner >> 1
    mirrored = jnp.zeros_like(rest)
    for b in range(row_bits - 1):
        mirrored = mirrored | (((rest >> b) & 1) << (row_bits - 2 - b))
    stream = inner >> (part.bit_length() - 1)
    route = jnp.where(stream & 1 == 1, rest, mirrored)
    target = ((stream << (row_bits - 1)) + route) * part + (inner & (part - 1))
    rel_col = ((global_cols & ((1 << span_bits) - 1)) >> nb_bits) ^ me_col
    phase, place = jnp.zeros_like(rel_col), jnp.zeros_like(rel_col)
    shards = [(p, rel) for p, rels in enumerate(arrival) for rel in rels]
    for at, (p, rel) in enumerate(shards):
        phase = jnp.where(rel_col == rel, p, phase)
        place = jnp.where(rel_col == rel, at, place)
    tile = (place << nb_bits) + (global_cols & (nb - 1))
    keep = len(arrival) + 1
    slot = lax.broadcasted_iota(jnp.int32, (1, slots), 1)
    key = jnp.where(owner & 1 == 0, jnp.where(phase == 0, keep - 1, keep), phase)
    key = jnp.where(slot < counts_ref[0, 0], key, keep + 1)
    key_order = key * slots + slot
    wide = plan_ref.shape[1]
    fill = jnp.zeros((1, wide - slots), jnp.int32)
    both = jnp.concatenate(
        [jnp.concatenate([x, fill], axis=1) for x in (key_order, slot, target, tile)] + [jnp.zeros((4, wide), jnp.int32)],
        axis=0,
    )
    columns = jnp.transpose(both.astype(jnp.float32))[:slots].astype(jnp.int32)
    rank = jnp.sum((key_order < columns[:, 0:1]).astype(jnp.int32), axis=1, keepdims=True)
    hit = rank == lax.broadcasted_iota(jnp.int32, (slots, wide), 1)
    for i in range(3):
        plan_ref[i : i + 1, :] = jnp.sum(jnp.where(hit, columns[:, i + 1 : i + 2], 0), axis=0, keepdims=True)
    lane = lax.broadcasted_iota(jnp.int32, (1, wide), 1)
    bounds = jnp.zeros((1, wide), jnp.int32)
    for k in range(1, keep + 2):
        bounds = jnp.where(lane == k, jnp.sum((key < k).astype(jnp.int32), axis=1, keepdims=True), bounds)
    plan_ref[3:4, :] = bounds
    plan_ref[4:8, :] = jnp.zeros((4, wide), jnp.int32)


def add_products(plan_ref, bucket, tiles, base, blocks_ref, acc_ref, ready=None):
    begin, end = plan_ref[3, bucket], plan_ref[3, bucket + 1]
    blank = tiles.shape[0] - 1

    def step(g, carry):
        if ready is not None:
            carry = ready(plan_ref[0, jnp.minimum(begin + g * GROUP + GROUP, end) - 1], carry)
        parts, targets = [], []
        for u in range(GROUP):
            at = begin + g * GROUP + u
            real = jnp.minimum(at, end - 1)
            left = tiles[jnp.where(at < end, plan_ref[2, real] - base, blank)]
            parts.append(
                lax.dot_general(
                    left, blocks_ref[plan_ref[0, real]], (((1,), (1,)), ((), ())), preferred_element_type=jnp.float32
                )
            )
            targets.append(plan_ref[1, real])
        for part, target in zip(parts, targets):
            acc_ref[target] += part
        return carry

    return lax.fori_loop(0, (end - begin + GROUP - 1) // GROUP, step, 0)


def fill_tiles(where, piece_refs, tiles):
    width = tiles.shape[2]
    for first, ref in zip(where, piece_refs):
        for i in range(ref.shape[1] // width):
            tiles[first + i] = ref[:, i * width : (i + 1) * width]
    tiles[tiles.shape[0] - 1] = jnp.zeros(tiles.shape[1:], tiles.dtype)


def first_kernel(where, arrival, nb, width_bits, rows_ref, cols_ref, counts_ref, *refs):
    piece_refs = refs[: len(where)]
    blocks_ref, acc_ref, store_ref, plan_ref, plan, tiles, rows, cols, sems, plan_sems = refs[len(where) :]
    chunks = sems.shape[0]
    size = blocks_ref.shape[0] // chunks

    def chunk(c):
        part = pl.ds(c * size, size)
        return pltpu.make_async_copy(blocks_ref.at[part], store_ref.at[part], sems.at[c])

    indices = [pltpu.make_async_copy(a, b, plan_sems.at[i]) for i, (a, b) in enumerate(((rows_ref, rows), (cols_ref, cols)))]
    for copy in indices:
        copy.start()
    for c in range(chunks):
        chunk(c).start()

    def wait(c, carry):
        chunk(c).wait()
        return carry

    def ready(slot, done):
        need = slot // size + 1
        lax.fori_loop(done, need, wait, 0)
        return jnp.maximum(done, need)

    fill_tiles(where, piece_refs, tiles)
    acc_ref[...] = jnp.zeros_like(acc_ref)
    for copy in indices:
        copy.wait()
    make_plan(arrival, nb, width_bits, rows, cols, counts_ref, plan_ref)
    to_scalar = pltpu.make_async_copy(plan_ref, plan, plan_sems.at[2])
    to_scalar.start()
    to_scalar.wait()
    done = add_products(plan, 0, tiles, 0, store_ref, acc_ref, ready)
    lax.fori_loop(done, chunks, wait, 0)


def multiply_first(block_rows, block_cols, counts, arrival, pieces, blocks, nb, rows, grid_rows, grid_cols):
    slots, width, _ = blocks.shape
    panel_cols = pieces[0][1].shape[0]
    bits = (nb.bit_length() - 1, (nb * grid_cols).bit_length() - 1, grid_rows.bit_length() - 1)
    vmem = pl.BlockSpec(memory_space=pltpu.VMEM)
    hbm = pl.BlockSpec(memory_space=pltpu.HBM)
    plan_shape = (8, -(-slots // 128) * 128)
    return pl.pallas_call(
        functools.partial(first_kernel, [first for first, _ in pieces], arrival, nb, bits),
        out_shape=(
            jax.ShapeDtypeStruct((rows, panel_cols, width), jnp.float32),
            jax.ShapeDtypeStruct(blocks.shape, blocks.dtype),
            jax.ShapeDtypeStruct(plan_shape, jnp.int32),
        ),
        in_specs=[hbm, hbm, pl.BlockSpec(memory_space=pltpu.SMEM)] + [vmem] * len(pieces) + [hbm],
        out_specs=(vmem, vmem, vmem),
        scratch_shapes=[
            pltpu.SMEM(plan_shape, jnp.int32),
            pltpu.VMEM((nb + 1, panel_cols, width), pieces[0][1].dtype),
            pltpu.VMEM(block_rows.shape, jnp.int32),
            pltpu.VMEM(block_cols.shape, jnp.int32),
            pltpu.SemaphoreType.DMA((CHUNKS,)),
            pltpu.SemaphoreType.DMA((3,)),
        ],
        compiler_params=pltpu.CompilerParams(vmem_limit_bytes=VMEM_LIMIT),
        cost_estimate=pl.CostEstimate(
            flops=slots // 8 * panel_cols * width * width * 2, bytes_accessed=2 * blocks.size, transcendentals=0
        ),
        name="multiply_first",
    )(
        pltpu.with_memory_space_constraint(block_rows, pltpu.HBM),
        pltpu.with_memory_space_constraint(block_cols, pltpu.HBM),
        counts,
        *[x for _, x in pieces],
        pltpu.with_memory_space_constraint(blocks, pltpu.HBM),
    )


def next_kernel(where, bucket, base, plan_ref, *refs):
    piece_refs = refs[: len(where)]
    blocks_ref = refs[len(where)]
    acc_ref, tiles = refs[-2:]
    fill_tiles(where, piece_refs, tiles)
    if len(refs) == len(where) + 3:
        acc_ref[...] = jnp.zeros_like(acc_ref)
    add_products(plan_ref, bucket, tiles, base, blocks_ref, acc_ref)


def multiply_next(plan, bucket, pieces, blocks, rows, total=None):
    panel_cols = pieces[0][1].shape[0]
    slots, width, _ = blocks.shape
    base = min(first for first, _ in pieces)
    tiles = sum(x.shape[1] for _, x in pieces) // width
    vmem = pl.BlockSpec(memory_space=pltpu.VMEM)
    operands = [plan, *[x for _, x in pieces], blocks] + ([] if total is None else [total])
    share = slots * len(pieces) // 16
    return pl.pallas_call(
        functools.partial(next_kernel, [first - base for first, _ in pieces], bucket, base),
        out_shape=jax.ShapeDtypeStruct((rows, panel_cols, width), jnp.float32),
        in_specs=[pl.BlockSpec(memory_space=pltpu.SMEM)] + [vmem] * (len(operands) - 1),
        out_specs=vmem,
        scratch_shapes=[pltpu.VMEM((tiles + 1, panel_cols, width), pieces[0][1].dtype)],
        input_output_aliases={} if total is None else {len(operands) - 1: 0},
        compiler_params=pltpu.CompilerParams(vmem_limit_bytes=VMEM_LIMIT),
        cost_estimate=pl.CostEstimate(
            flops=share * panel_cols * width * width * 2, bytes_accessed=share * width * width * 2, transcendentals=0
        ),
        name="multiply_next",
    )(*operands)


def encode(rows, out_ref):
    shape = rows[0].shape
    lane = lax.broadcasted_iota(jnp.int32, shape, 1)
    scales = jnp.zeros(shape, jnp.int32)
    for i, row in enumerate(rows):
        top = jnp.max(jnp.abs(row), axis=1, keepdims=True)
        code = jnp.ceil(jnp.log2(jnp.maximum(top, 2.0**-100)) * 128.0) + 1.0
        out_ref[i] = jnp.round(row * jnp.exp2(15.0 - code / 128.0)).astype(jnp.int32).astype(jnp.int16)
        scales = jnp.where(lane == i, jnp.broadcast_to(code.astype(jnp.int32), shape), scales)
    out_ref[len(rows)] = scales.astype(jnp.int16)


def decode(ref):
    n, shape = ref.shape[0] - 1, ref.shape[1:]
    steps = jnp.exp2(ref[n].astype(jnp.int32).astype(jnp.float32) / 128.0 - 15.0)
    return lambda i: ref[i].astype(jnp.int32).astype(jnp.float32) * jnp.broadcast_to(steps[:, i : i + 1], shape)


def reader(ref):
    return decode(ref) if ref.dtype == jnp.int16 else lambda i: ref[i]


def split_kernel(a_ref, b_ref, *outs):
    got = reader(b_ref)
    at = 0
    for keep_ref, send_ref in zip(outs[0::2], outs[1::2]):
        n = keep_ref.shape[0]
        for i in range(n):
            keep_ref[i] = a_ref[at + i] + got(at + i)
        encode([a_ref[at + n + i] + got(at + n + i) for i in range(n)], send_ref)
        at += 2 * n


def add_and_split(a, b, pairs):
    n, rest = a.shape[0] // (2 * pairs), a.shape[1:]
    vmem = pl.BlockSpec(memory_space=pltpu.VMEM)
    return pl.pallas_call(
        split_kernel,
        out_shape=[jax.ShapeDtypeStruct((n,) + rest, a.dtype), jax.ShapeDtypeStruct((n + 1,) + rest, jnp.int16)] * pairs,
        in_specs=[vmem, vmem],
        out_specs=[vmem] * (2 * pairs),
        compiler_params=pltpu.CompilerParams(vmem_limit_bytes=VMEM_LIMIT),
        name="add_and_split",
    )(a, b)


def spread_kernel(streams, a_ref, b_ref, *outs):
    got = reader(b_ref)
    n = outs[0].shape[0]
    for k in range(streams):
        for i, out in enumerate(outs[4 * k : 4 * k + 4]):
            at = (4 * k + i) * n
            rows = [a_ref[at + j] + got(at + j) for j in range(n)]
            if i < 2:
                for j in range(n):
                    out[j] = rows[j]
            else:
                encode(rows, out)


def spread(a, b, streams):
    n, rest = a.shape[0] // (4 * streams), a.shape[1:]
    vmem = pl.BlockSpec(memory_space=pltpu.VMEM)
    plain, coded = jax.ShapeDtypeStruct((n,) + rest, a.dtype), jax.ShapeDtypeStruct((n + 1,) + rest, jnp.int16)
    outs = pl.pallas_call(
        functools.partial(spread_kernel, streams),
        out_shape=[plain, plain, coded, coded] * streams,
        in_specs=[vmem, vmem],
        out_specs=[vmem] * (4 * streams),
        compiler_params=pltpu.CompilerParams(vmem_limit_bytes=VMEM_LIMIT),
        name="spread",
    )(a, b)
    return [outs[4 * k : 4 * k + 4] for k in range(streams)]


def relay_kernel(a_ref, b_ref, out_ref):
    got = reader(b_ref)
    encode([a_ref[i] + got(i) for i in range(a_ref.shape[0])], out_ref)


def relay(a, b):
    vmem = pl.BlockSpec(memory_space=pltpu.VMEM)
    return pl.pallas_call(
        relay_kernel,
        out_shape=jax.ShapeDtypeStruct(b.shape, b.dtype),
        in_specs=[vmem, vmem],
        out_specs=vmem,
        compiler_params=pltpu.CompilerParams(vmem_limit_bytes=VMEM_LIMIT),
        name="relay",
    )(a, b)


def split3(x):
    high = x.astype(jnp.bfloat16)
    rest = x - high.astype(jnp.float32)
    middle = rest.astype(jnp.bfloat16)
    return high, middle, (rest - middle.astype(jnp.float32)).astype(jnp.bfloat16)


def gram_kernel(*refs):
    ins, (stack_ref, gram_ref) = refs[:-2], refs[-2:]
    s = ins[0].shape[1]
    products = jnp.zeros((3 * s, 3 * s), jnp.float32)
    pieces = [(a, reader(b), reader(c), i) for a, b, c in zip(*(ins[k::3] for k in range(3))) for i in range(a.shape[0])]
    for at in range(0, len(pieces), 2):
        stacks = []
        for k in (0, 1):
            a, b, c, i = pieces[at + k]
            stack = jnp.concatenate(split3(a[i] + b(i) + c(i)), axis=0)
            stack_ref[at + k] = stack
            stacks.append(stack)
        both = jnp.concatenate(stacks, axis=1)
        products += lax.dot_general(both, both, (((1,), (1,)), ((), ())), preferred_element_type=jnp.float32)
    gram = jnp.zeros((s, s), jnp.float32)
    for i in range(3):
        for j in range(3 - i):
            gram += products[i * s : (i + 1) * s, j * s : (j + 1) * s]
    height = gram_ref.shape[1]
    packed = jnp.concatenate([gram[i : i + height] for i in range(0, s, height)], axis=1)
    for i in range(gram_ref.shape[0]):
        gram_ref[i] = packed


def gram_of(terms, copies):
    vmem = pl.BlockSpec(memory_space=pltpu.VMEM)
    flat = [x for term in terms for x in term]
    _, s, width = flat[0].shape
    rows = sum(term[0].shape[0] for term in terms)
    return pl.pallas_call(
        gram_kernel,
        out_shape=(
            jax.ShapeDtypeStruct((rows, 3 * s, width), jnp.bfloat16),
            jax.ShapeDtypeStruct((copies, s * s // width, width), jnp.float32),
        ),
        in_specs=[vmem] * len(flat),
        out_specs=[vmem, vmem],
        compiler_params=pltpu.CompilerParams(vmem_limit_bytes=VMEM_LIMIT),
        name="gram",
    )(*flat)


def factor_kernel(total_rows, grams_ref, stack_ref, basis_ref, factor_ref):
    s = factor_ref.shape[0]
    width = grams_ref.shape[2]
    packed = jnp.sum(grams_ref[...], axis=0) / total_rows
    gram = jnp.concatenate([packed[:, i : i + s] for i in range(0, width, s)], axis=0)
    ri = lax.broadcasted_iota(jnp.int32, (s, width), 0)
    ci = lax.broadcasted_iota(jnp.int32, (s, width), 1)
    unit = jnp.where(ri == ci, 1.0, 0.0).astype(jnp.float32)[:, :s]
    work = jnp.concatenate([gram, unit, jnp.zeros((s, width - 2 * s), jnp.float32)], axis=1)
    pivots = jnp.ones((s, width), jnp.float32)
    spread = lambda x: jnp.broadcast_to(x, (s, width))
    for j in range(0, s, 2):
        k = j + 1
        first, cross, second = spread(work[j:k, j:k]), spread(work[k : k + 1, j:k]), spread(work[k : k + 1, k : k + 1])
        row1, row2 = spread(work[j:k, :]), spread(work[k : k + 1, :])
        col1, col2 = spread(work[:, j:k]), spread(work[:, k : k + 1])
        ratio = cross / first
        second = second - cross * ratio
        row2 = row2 - ratio * row1
        col2 = col2 - ratio * col1
        reduced = work - col1 * (row1 / first) - col2 * (row2 / second)
        work = jnp.where(ri > k, reduced, jnp.where(ri == k, row2, work))
        pivots = jnp.where(ri == j, first, jnp.where(ri == k, second, pivots))
    work = work * lax.rsqrt(pivots)
    factor_ref[...] = jnp.where(ci >= ri, work, 0.0)[:, :s]
    high, middle, low = split3(work[:, s : 2 * s])
    left = jnp.concatenate([high, high, high, middle, middle, low], axis=1)
    for i in range(0, stack_ref.shape[0], 2):
        both = jnp.concatenate([stack_ref[i], stack_ref[i + 1]], axis=1)
        right = jnp.concatenate([both, both[: 2 * s], both[:s]], axis=0)
        basis_ref[:, i * width : (i + 2) * width] = jnp.dot(
            left, right, preferred_element_type=jnp.float32
        ).astype(basis_ref.dtype)


def finish(grams, stack, total_rows):
    vmem = pl.BlockSpec(memory_space=pltpu.VMEM)
    n, rows3, width = stack.shape
    s = rows3 // 3
    return pl.pallas_call(
        functools.partial(factor_kernel, total_rows),
        out_shape=(
            jax.ShapeDtypeStruct((s, n * width), jnp.bfloat16),
            jax.ShapeDtypeStruct((s, s), jnp.float32),
        ),
        in_specs=[vmem, vmem],
        out_specs=[vmem, vmem],
        compiler_params=pltpu.CompilerParams(vmem_limit_bytes=VMEM_LIMIT),
        name="finish",
    )(grams, stack)


def on_device(blocks, block_rows, block_cols, counts, panel):
    width = blocks.shape[-1]
    nb = panel.shape[1] // width
    grid_rows = lax.axis_size("row")
    grid_cols = lax.axis_size("col")
    bits = grid_rows.bit_length() - 1
    rows = grid_rows * nb // 2

    own, near = near_pieces(panel, grid_cols)
    arrival = [[0], list(dict.fromkeys(rel for rel, _, _ in near))] + ([[2]] if grid_cols == 4 else [])
    order = [rel for rels in arrival for rel in rels]
    number = lambda pieces: [(order.index(rel) * nb + column // width, x) for rel, column, x in pieces]

    send, store, plan = multiply_first(
        block_rows, block_cols, counts, arrival, number(own), blocks[0, 0], nb, rows, grid_rows, grid_cols
    )
    phases = [own, near]
    if grid_cols == 4:
        first, second, send = lax.optimization_barrier((near[0][2], near[1][2], send))
        phases.append(opposite_pieces(first, second))
    phases = [number(pieces) for pieces in phases]
    send = multiply_next(plan, 1, phases[1], store, rows, total=send)
    keep = multiply_next(plan, len(phases), phases[0], store, rows)
    if grid_cols == 4:
        (tile0, cross0), (tile1, cross1) = phases[2]
        cross0, cross1, keep = lax.optimization_barrier((cross0, cross1, keep))
        phases[2] = [(tile0, cross0), (tile1, cross1)]
        send = multiply_next(plan, 2, phases[2], store, rows, total=send)
    got = lax.ppermute(send, "row", flips(grid_rows, 1))
    rest = [piece for pieces in phases[1:] for piece in pieces]
    keep = multiply_next(plan, len(phases) + 1, rest, store, rows, total=keep)

    move = lambda x, i, stage: lax.ppermute(x, "row", flips(grid_rows, 1 << (bits - stage if i % 2 else stage)))
    if bits > 3:
        parts = add_and_split(keep, got, STREAMS)
        streams = [(parts[2 * i], move(parts[2 * i + 1], i, 1)) for i in range(STREAMS)]
        for stage in range(2, bits - 2):
            parts = [add_and_split(kept, x, 1) for kept, x in streams]
            streams = [(kept, move(x, i, stage)) for i, (kept, x) in enumerate(parts)]
        streams = [spread(kept, x, 1)[0] for kept, x in streams]
    else:
        streams = spread(keep, got, STREAMS)
    far = [move(stream[3], i, bits - 2) for i, stream in enumerate(streams)]
    near = [move(stream[2], i, bits - 2) for i, stream in enumerate(streams)]
    last = [move(relay(stream[1], x), i, bits - 1) for i, (stream, x) in enumerate(zip(streams, far))]
    streams = [(stream[0], x, y) for stream, x, y in zip(streams, near, last)]

    devices = grid_rows * grid_cols
    stack, grams = gram_of(streams, devices)
    grams = lax.all_to_all(grams, ("row", "col"), 0, 0, tiled=True)
    return finish(grams, stack, nb * width * devices)


def solution(mesh):
    in_specs = (
        P("row", "col", None, None, None),
        P("row", "col", None),
        P("row", "col", None),
        P("row", "col"),
        P(None, ("row", "col")),
    )
    out_specs = (P(None, ("row", "col")), P())
    return jax.shard_map(
        on_device, mesh=mesh, in_specs=in_specs, out_specs=out_specs, check_vma=False
    )
```

```python
import functools

import jax
import jax.numpy as jnp
from jax import lax
from jax.experimental import pallas as pl
from jax.experimental.pallas import tpu as pltpu
from jax.sharding import PartitionSpec as P

GROUP = 32
STREAMS = 2
VMEM_LIMIT = 16 << 20
CHUNKS = 10
PIVOTS = 8


def flips(size, mask):
    return [(i, i ^ mask) for i in range(size)]


def near_pieces(panel, size):
    cols = panel.shape[1]
    if size != 4:
        held = [(0, panel)]
        bit = 1
        while bit < size:
            held = held + [(rel ^ bit, lax.ppermute(x, "col", flips(size, bit))) for rel, x in held]
            bit *= 2
        return [(0, 0, panel)], [(rel, 0, x) for rel, x in held[1:]]
    near = lax.ppermute(panel, "col", flips(4, 1))
    half = cols // 2
    low, high = panel[:, :half], panel[:, half:]
    far_low = lax.ppermute(low, "col", flips(4, 3))
    far_high = lax.ppermute(high, "col", flips(4, 3))
    return [(0, 0, low), (0, half, high)], [(1, 0, near), (3, 0, far_low), (3, half, far_high)]


def opposite_pieces(near, far_low):
    half = far_low.shape[1]
    cross_low = lax.ppermute(far_low, "col", flips(4, 1))
    cross_high = lax.ppermute(near[:, half:], "col", flips(4, 3))
    return [(2, 0, cross_low), (2, half, cross_high)]


def make_plan(arrival, nb, width_bits, rows_ref, cols_ref, counts_ref, plan_ref):
    slots = rows_ref.shape[-1]
    nb_bits, span_bits, row_bits = width_bits
    part = nb // STREAMS
    me_row, me_col = lax.axis_index("row"), lax.axis_index("col")
    global_rows, global_cols = rows_ref[0], cols_ref[0]
    owner = (global_rows >> span_bits) ^ me_row
    inner = global_rows & (nb - 1)
    rest = owner >> 1
    mirrored = jnp.zeros_like(rest)
    for b in range(row_bits - 1):
        mirrored = mirrored | (((rest >> b) & 1) << (row_bits - 2 - b))
    stream = inner >> (part.bit_length() - 1)
    route = jnp.where(stream & 1 == 1, rest, mirrored)
    target = ((stream << (row_bits - 1)) + route) * part + (inner & (part - 1))
    rel_col = ((global_cols & ((1 << span_bits) - 1)) >> nb_bits) ^ me_col
    phase, place = jnp.zeros_like(rel_col), jnp.zeros_like(rel_col)
    shards = [(p, rel) for p, rels in enumerate(arrival) for rel in rels]
    for at, (p, rel) in enumerate(shards):
        phase = jnp.where(rel_col == rel, p, phase)
        place = jnp.where(rel_col == rel, at, place)
    tile = (place << nb_bits) + (global_cols & (nb - 1))
    keep = len(arrival) + 1
    slot = lax.broadcasted_iota(jnp.int32, (1, slots), 1)
    key = jnp.where(owner & 1 == 0, jnp.where(phase == 0, keep - 1, keep), phase)
    key = jnp.where(slot < counts_ref[0, 0], key, keep + 1)
    key_order = key * slots + slot
    wide = plan_ref.shape[1]
    fill = jnp.zeros((1, wide - slots), jnp.int32)
    both = jnp.concatenate(
        [jnp.concatenate([x, fill], axis=1) for x in (key_order, slot, target, tile)] + [jnp.zeros((4, wide), jnp.int32)],
        axis=0,
    )
    columns = jnp.transpose(both.astype(jnp.float32))[:slots].astype(jnp.int32)
    rank = jnp.sum((key_order < columns[:, 0:1]).astype(jnp.int32), axis=1, keepdims=True)
    hit = rank == lax.broadcasted_iota(jnp.int32, (slots, wide), 1)
    for i in range(3):
        plan_ref[i : i + 1, :] = jnp.sum(jnp.where(hit, columns[:, i + 1 : i + 2], 0), axis=0, keepdims=True)
    lane = lax.broadcasted_iota(jnp.int32, (1, wide), 1)
    bounds = jnp.zeros((1, wide), jnp.int32)
    for k in range(1, keep + 2):
        bounds = jnp.where(lane == k, jnp.sum((key < k).astype(jnp.int32), axis=1, keepdims=True), bounds)
    plan_ref[3:4, :] = bounds
    plan_ref[4:8, :] = jnp.zeros((4, wide), jnp.int32)


def add_products(plan_ref, bucket, tiles, base, blocks_ref, acc_ref, ready=None, done=0):
    begin, end = plan_ref[3, bucket], plan_ref[3, bucket + 1]
    blank = tiles.shape[0] - 1

    def step(g, carry):
        if ready is not None:
            carry = ready(plan_ref[0, jnp.minimum(begin + g * GROUP + GROUP, end) - 1], carry)
        parts, targets = [], []
        for u in range(GROUP):
            at = begin + g * GROUP + u
            real = jnp.minimum(at, end - 1)
            left = tiles[jnp.where(at < end, plan_ref[2, real] - base, blank)]
            parts.append(
                lax.dot_general(
                    left, blocks_ref[plan_ref[0, real]], (((1,), (1,)), ((), ())), preferred_element_type=jnp.float32
                )
            )
            targets.append(plan_ref[1, real])
        for part, target in zip(parts, targets):
            acc_ref[target] += part
        return carry

    return lax.fori_loop(0, (end - begin + GROUP - 1) // GROUP, step, done)


def fill_tiles(where, piece_refs, tiles):
    width = tiles.shape[2]
    for first, ref in zip(where, piece_refs):
        for i in range(ref.shape[1] // width):
            tiles[first + i] = ref[:, i * width : (i + 1) * width]
    tiles[tiles.shape[0] - 1] = jnp.zeros(tiles.shape[1:], tiles.dtype)


def first_kernel(where, arrival, nb, width_bits, rows_ref, cols_ref, counts_ref, *refs):
    piece_refs = refs[: len(where)]
    blocks_ref, acc_ref, keep_ref, store_ref, plan_ref, plan, tiles, rows, cols, sems, plan_sems = refs[len(where) :]
    chunks = sems.shape[0]
    size = blocks_ref.shape[0] // chunks

    def chunk(c):
        part = pl.ds(c * size, size)
        return pltpu.make_async_copy(blocks_ref.at[part], store_ref.at[part], sems.at[c])

    indices = [pltpu.make_async_copy(a, b, plan_sems.at[i]) for i, (a, b) in enumerate(((rows_ref, rows), (cols_ref, cols)))]
    for copy in indices:
        copy.start()
    for copy in indices:
        copy.wait()
    for c in range(chunks):
        chunk(c).start()

    def wait(c, carry):
        chunk(c).wait()
        return carry

    def ready(slot, done):
        need = slot // size + 1
        lax.fori_loop(done, need, wait, 0)
        return jnp.maximum(done, need)

    fill_tiles(where, piece_refs, tiles)
    acc_ref[...] = jnp.zeros_like(acc_ref)
    keep_ref[...] = jnp.zeros_like(keep_ref)
    make_plan(arrival, nb, width_bits, rows, cols, counts_ref, plan_ref)
    to_scalar = pltpu.make_async_copy(plan_ref, plan, plan_sems.at[2])
    to_scalar.start()
    to_scalar.wait()
    done = add_products(plan, 0, tiles, 0, store_ref, acc_ref, ready)
    done = add_products(plan, len(arrival), tiles, 0, store_ref, keep_ref, ready, done)
    lax.fori_loop(done, chunks, wait, 0)


def multiply_first(block_rows, block_cols, counts, arrival, pieces, blocks, nb, rows, grid_rows, grid_cols):
    slots, width, _ = blocks.shape
    panel_cols = pieces[0][1].shape[0]
    bits = (nb.bit_length() - 1, (nb * grid_cols).bit_length() - 1, grid_rows.bit_length() - 1)
    vmem = pl.BlockSpec(memory_space=pltpu.VMEM)
    hbm = pl.BlockSpec(memory_space=pltpu.HBM)
    plan_shape = (8, -(-slots // 128) * 128)
    return pl.pallas_call(
        functools.partial(first_kernel, [first for first, _ in pieces], arrival, nb, bits),
        out_shape=(
            jax.ShapeDtypeStruct((rows, panel_cols, width), jnp.float32),
            jax.ShapeDtypeStruct((rows, panel_cols, width), jnp.float32),
            jax.ShapeDtypeStruct(blocks.shape, blocks.dtype),
            jax.ShapeDtypeStruct(plan_shape, jnp.int32),
        ),
        in_specs=[hbm, hbm, pl.BlockSpec(memory_space=pltpu.SMEM)] + [vmem] * len(pieces) + [hbm],
        out_specs=(vmem, vmem, vmem, vmem),
        scratch_shapes=[
            pltpu.SMEM(plan_shape, jnp.int32),
            pltpu.VMEM((nb + 1, panel_cols, width), pieces[0][1].dtype),
            pltpu.VMEM(block_rows.shape, jnp.int32),
            pltpu.VMEM(block_cols.shape, jnp.int32),
            pltpu.SemaphoreType.DMA((CHUNKS,)),
            pltpu.SemaphoreType.DMA((3,)),
        ],
        compiler_params=pltpu.CompilerParams(vmem_limit_bytes=VMEM_LIMIT),
        cost_estimate=pl.CostEstimate(
            flops=slots // 8 * panel_cols * width * width * 2, bytes_accessed=2 * blocks.size, transcendentals=0
        ),
        name="multiply_first",
    )(
        pltpu.with_memory_space_constraint(block_rows, pltpu.HBM),
        pltpu.with_memory_space_constraint(block_cols, pltpu.HBM),
        counts,
        *[x for _, x in pieces],
        pltpu.with_memory_space_constraint(blocks, pltpu.HBM),
    )


def next_kernel(where, bucket, base, plan_ref, *refs):
    piece_refs = refs[: len(where)]
    blocks_ref = refs[len(where)]
    acc_ref, tiles = refs[-2:]
    fill_tiles(where, piece_refs, tiles)
    if len(refs) == len(where) + 3:
        acc_ref[...] = jnp.zeros_like(acc_ref)
    add_products(plan_ref, bucket, tiles, base, blocks_ref, acc_ref)


def multiply_next(plan, bucket, pieces, blocks, rows, total=None):
    panel_cols = pieces[0][1].shape[0]
    slots, width, _ = blocks.shape
    base = min(first for first, _ in pieces)
    tiles = sum(x.shape[1] for _, x in pieces) // width
    vmem = pl.BlockSpec(memory_space=pltpu.VMEM)
    operands = [plan, *[x for _, x in pieces], blocks] + ([] if total is None else [total])
    share = slots * len(pieces) // 16
    return pl.pallas_call(
        functools.partial(next_kernel, [first - base for first, _ in pieces], bucket, base),
        out_shape=jax.ShapeDtypeStruct((rows, panel_cols, width), jnp.float32),
        in_specs=[pl.BlockSpec(memory_space=pltpu.SMEM)] + [vmem] * (len(operands) - 1),
        out_specs=vmem,
        scratch_shapes=[pltpu.VMEM((tiles + 1, panel_cols, width), pieces[0][1].dtype)],
        input_output_aliases={} if total is None else {len(operands) - 1: 0},
        compiler_params=pltpu.CompilerParams(vmem_limit_bytes=VMEM_LIMIT),
        cost_estimate=pl.CostEstimate(
            flops=share * panel_cols * width * width * 2, bytes_accessed=share * width * width * 2, transcendentals=0
        ),
        name="multiply_next",
    )(*operands)


def encode(rows, out_ref):
    shape = rows[0].shape
    lane = lax.broadcasted_iota(jnp.int32, shape, 1)
    scales = jnp.zeros(shape, jnp.int32)
    for i, row in enumerate(rows):
        top = jnp.max(jnp.abs(row), axis=1, keepdims=True)
        code = jnp.ceil(jnp.log2(jnp.maximum(top, 2.0**-100)) * 128.0) + 1.0
        out_ref[i] = jnp.round(row * jnp.exp2(15.0 - code / 128.0)).astype(jnp.int32).astype(jnp.int16)
        scales = jnp.where(lane == i, jnp.broadcast_to(code.astype(jnp.int32), shape), scales)
    out_ref[len(rows)] = scales.astype(jnp.int16)


def decode(ref):
    n, shape = ref.shape[0] - 1, ref.shape[1:]
    steps = jnp.exp2(ref[n].astype(jnp.int32).astype(jnp.float32) / 128.0 - 15.0)
    return lambda i: ref[i].astype(jnp.int32).astype(jnp.float32) * jnp.broadcast_to(steps[:, i : i + 1], shape)


def reader(ref):
    return decode(ref) if ref.dtype == jnp.int16 else lambda i: ref[i]


def split_kernel(a_ref, b_ref, *outs):
    got = reader(b_ref)
    at = 0
    for keep_ref, send_ref in zip(outs[0::2], outs[1::2]):
        n = keep_ref.shape[0]
        for i in range(n):
            keep_ref[i] = a_ref[at + i] + got(at + i)
        encode([a_ref[at + n + i] + got(at + n + i) for i in range(n)], send_ref)
        at += 2 * n


def add_and_split(a, b, pairs):
    n, rest = a.shape[0] // (2 * pairs), a.shape[1:]
    vmem = pl.BlockSpec(memory_space=pltpu.VMEM)
    return pl.pallas_call(
        split_kernel,
        out_shape=[jax.ShapeDtypeStruct((n,) + rest, a.dtype), jax.ShapeDtypeStruct((n + 1,) + rest, jnp.int16)] * pairs,
        in_specs=[vmem, vmem],
        out_specs=[vmem] * (2 * pairs),
        compiler_params=pltpu.CompilerParams(vmem_limit_bytes=VMEM_LIMIT),
        name="add_and_split",
    )(a, b)


def spread_kernel(streams, a_ref, b_ref, *outs):
    got = reader(b_ref)
    n = outs[0].shape[0]
    for k in range(streams):
        for i, out in enumerate(outs[4 * k : 4 * k + 4]):
            at = (4 * k + i) * n
            rows = [a_ref[at + j] + got(at + j) for j in range(n)]
            if i < 2:
                for j in range(n):
                    out[j] = rows[j]
            else:
                encode(rows, out)


def spread(a, b, streams):
    n, rest = a.shape[0] // (4 * streams), a.shape[1:]
    vmem = pl.BlockSpec(memory_space=pltpu.VMEM)
    plain, coded = jax.ShapeDtypeStruct((n,) + rest, a.dtype), jax.ShapeDtypeStruct((n + 1,) + rest, jnp.int16)
    outs = pl.pallas_call(
        functools.partial(spread_kernel, streams),
        out_shape=[plain, plain, coded, coded] * streams,
        in_specs=[vmem, vmem],
        out_specs=[vmem] * (4 * streams),
        compiler_params=pltpu.CompilerParams(vmem_limit_bytes=VMEM_LIMIT),
        name="spread",
    )(a, b)
    return [outs[4 * k : 4 * k + 4] for k in range(streams)]


def relay_kernel(a_ref, b_ref, out_ref):
    got = reader(b_ref)
    encode([a_ref[i] + got(i) for i in range(a_ref.shape[0])], out_ref)


def relay(a, b):
    vmem = pl.BlockSpec(memory_space=pltpu.VMEM)
    return pl.pallas_call(
        relay_kernel,
        out_shape=jax.ShapeDtypeStruct(b.shape, b.dtype),
        in_specs=[vmem, vmem],
        out_specs=vmem,
        compiler_params=pltpu.CompilerParams(vmem_limit_bytes=VMEM_LIMIT),
        name="relay",
    )(a, b)


def split3(x):
    high = x.astype(jnp.bfloat16)
    rest = x - high.astype(jnp.float32)
    middle = rest.astype(jnp.bfloat16)
    return high, middle, (rest - middle.astype(jnp.float32)).astype(jnp.bfloat16)


def gram_kernel(*refs):
    ins, (stack_ref, gram_ref) = refs[:-2], refs[-2:]
    s = ins[0].shape[1]
    products = jnp.zeros((3 * s, 3 * s), jnp.float32)
    pieces = [(a, reader(b), reader(c), i) for a, b, c in zip(*(ins[k::3] for k in range(3))) for i in range(a.shape[0])]
    for at in range(0, len(pieces), 2):
        stacks = []
        for k in (0, 1):
            a, b, c, i = pieces[at + k]
            stack = jnp.concatenate(split3(a[i] + b(i) + c(i)), axis=0)
            stack_ref[at + k] = stack
            stacks.append(stack)
        both = jnp.concatenate(stacks, axis=1)
        products += lax.dot_general(both, both, (((1,), (1,)), ((), ())), preferred_element_type=jnp.float32)
    gram = jnp.zeros((s, s), jnp.float32)
    for i in range(3):
        for j in range(3 - i):
            gram += products[i * s : (i + 1) * s, j * s : (j + 1) * s]
    height = gram_ref.shape[1]
    packed = jnp.concatenate([gram[i : i + height] for i in range(0, s, height)], axis=1)
    for i in range(gram_ref.shape[0]):
        gram_ref[i] = packed


def gram_of(terms, copies):
    vmem = pl.BlockSpec(memory_space=pltpu.VMEM)
    flat = [x for term in terms for x in term]
    _, s, width = flat[0].shape
    rows = sum(term[0].shape[0] for term in terms)
    return pl.pallas_call(
        gram_kernel,
        out_shape=(
            jax.ShapeDtypeStruct((rows, 3 * s, width), jnp.bfloat16),
            jax.ShapeDtypeStruct((copies, s * s // width, width), jnp.float32),
        ),
        in_specs=[vmem] * len(flat),
        out_specs=[vmem, vmem],
        compiler_params=pltpu.CompilerParams(vmem_limit_bytes=VMEM_LIMIT),
        name="gram",
    )(*flat)


def factor_kernel(total_rows, grams_ref, stack_ref, basis_ref, factor_ref):
    s = factor_ref.shape[0]
    width = grams_ref.shape[2]
    packed = jnp.sum(grams_ref[...], axis=0) / total_rows
    gram = jnp.concatenate([packed[:, i : i + s] for i in range(0, width, s)], axis=0)
    ri = lax.broadcasted_iota(jnp.int32, (s, width), 0)
    ci = lax.broadcasted_iota(jnp.int32, (s, width), 1)
    unit = jnp.where(ri == ci, 1.0, 0.0).astype(jnp.float32)[:, :s]
    work = jnp.concatenate([gram, unit, jnp.zeros((s, width - 2 * s), jnp.float32)], axis=1)
    pivots = jnp.ones((s, width), jnp.float32)
    flat = lambda x: jnp.broadcast_to(x, (8, width))
    tall = lambda x: jnp.concatenate([x] * (s // 8), axis=0)
    for j in range(0, s, PIVOTS):
        rows = [flat(work[j + p : j + p + 1, :]) for p in range(PIVOTS)]
        columns = [jnp.broadcast_to(work[:, j + p : j + p + 1], (s, width)) for p in range(PIVOTS)]
        entry = [[flat(work[j + p : j + p + 1, j + q : j + q + 1]) for q in range(PIVOTS)] for p in range(PIVOTS)]
        units = []
        for p in range(PIVOTS):
            inverse = 1.0 / entry[p][p]
            units.append(rows[p] * inverse)
            ratio = [entry[p][q] * inverse for q in range(PIVOTS)]
            for q in range(p + 1, PIVOTS):
                rows[q] = rows[q] - entry[p][q] * units[p]
                columns[q] = columns[q] - columns[p] * tall(ratio[q])
                for t in range(q, PIVOTS):
                    entry[q][t] = entry[q][t] - entry[p][q] * ratio[t]
        reduced = work
        for p in range(PIVOTS):
            reduced = reduced - columns[p] * tall(units[p])
        work = jnp.where(ri >= j + PIVOTS, reduced, work)
        for p in range(PIVOTS):
            work = jnp.where(ri == j + p, tall(rows[p]), work)
            pivots = jnp.where(ri == j + p, tall(entry[p][p]), pivots)
    work = work * lax.rsqrt(pivots)
    factor_ref[...] = jnp.where(ci >= ri, work, 0.0)[:, :s]
    high, middle, low = split3(work[:, s : 2 * s])
    left = jnp.concatenate([high, high, high, middle, middle, low], axis=1)
    for i in range(0, stack_ref.shape[0], 2):
        both = jnp.concatenate([stack_ref[i], stack_ref[i + 1]], axis=1)
        right = jnp.concatenate([both, both[: 2 * s], both[:s]], axis=0)
        basis_ref[:, i * width : (i + 2) * width] = jnp.dot(
            left, right, preferred_element_type=jnp.float32
        ).astype(basis_ref.dtype)


def finish(grams, stack, total_rows):
    vmem = pl.BlockSpec(memory_space=pltpu.VMEM)
    n, rows3, width = stack.shape
    s = rows3 // 3
    return pl.pallas_call(
        functools.partial(factor_kernel, total_rows),
        out_shape=(
            jax.ShapeDtypeStruct((s, n * width), jnp.bfloat16),
            jax.ShapeDtypeStruct((s, s), jnp.float32),
        ),
        in_specs=[vmem, vmem],
        out_specs=[vmem, vmem],
        compiler_params=pltpu.CompilerParams(vmem_limit_bytes=VMEM_LIMIT),
        name="finish",
    )(grams, stack)


def on_device(blocks, block_rows, block_cols, counts, panel):
    width = blocks.shape[-1]
    nb = panel.shape[1] // width
    grid_rows = lax.axis_size("row")
    grid_cols = lax.axis_size("col")
    bits = grid_rows.bit_length() - 1
    rows = grid_rows * nb // 2

    own, near = near_pieces(panel, grid_cols)
    arrival = [[0], list(dict.fromkeys(rel for rel, _, _ in near))] + ([[2]] if grid_cols == 4 else [])
    order = [rel for rels in arrival for rel in rels]
    number = lambda pieces: [(order.index(rel) * nb + column // width, x) for rel, column, x in pieces]

    send, keep, store, plan = multiply_first(
        block_rows, block_cols, counts, arrival, number(own), blocks[0, 0], nb, rows, grid_rows, grid_cols
    )
    phases = [own, near]
    if grid_cols == 4:
        first, second, send = lax.optimization_barrier((near[0][2], near[1][2], send))
        phases.append(opposite_pieces(first, second))
    phases = [number(pieces) for pieces in phases]
    send = multiply_next(plan, 1, phases[1], store, rows, total=send)
    if grid_cols == 4:
        send = multiply_next(plan, 2, phases[2], store, rows, total=send)
    got = lax.ppermute(send, "row", flips(grid_rows, 1))
    rest = [piece for pieces in phases[1:] for piece in pieces]
    keep = multiply_next(plan, len(phases) + 1, rest, store, rows, total=keep)

    move = lambda x, i, stage: lax.ppermute(x, "row", flips(grid_rows, 1 << (bits - stage if i % 2 else stage)))
    if bits > 3:
        parts = add_and_split(keep, got, STREAMS)
        streams = [(parts[2 * i], move(parts[2 * i + 1], i, 1)) for i in range(STREAMS)]
        for stage in range(2, bits - 2):
            parts = [add_and_split(kept, x, 1) for kept, x in streams]
            streams = [(kept, move(x, i, stage)) for i, (kept, x) in enumerate(parts)]
        streams = [spread(kept, x, 1)[0] for kept, x in streams]
    else:
        streams = spread(keep, got, STREAMS)
    far = [move(stream[3], i, bits - 2) for i, stream in enumerate(streams)]
    near = [move(stream[2], i, bits - 2) for i, stream in enumerate(streams)]
    last = [move(relay(stream[1], x), i, bits - 1) for i, (stream, x) in enumerate(zip(streams, far))]
    streams = [(stream[0], x, y) for stream, x, y in zip(streams, near, last)]

    devices = grid_rows * grid_cols
    stack, grams = gram_of(streams, devices)
    grams = lax.all_to_all(grams, ("row", "col"), 0, 0, tiled=True)
    return finish(grams, stack, nb * width * devices)


def solution(mesh):
    in_specs = (
        P("row", "col", None, None, None),
        P("row", "col", None),
        P("row", "col", None),
        P("row", "col"),
        P(None, ("row", "col")),
    )
    out_specs = (P(None, ("row", "col")), P())
    return jax.shard_map(
        on_device, mesh=mesh, in_specs=in_specs, out_specs=out_specs, check_vma=False
    )
```

```python
import functools

import jax
import jax.numpy as jnp
from jax import lax
from jax.experimental import pallas as pl
from jax.experimental.pallas import tpu as pltpu
from jax.sharding import PartitionSpec as P

GROUP = 32
STREAMS = 2
VMEM_LIMIT = 16 << 20
CHUNKS = 10
PIVOTS = 8


def flips(size, mask):
    return [(i, i ^ mask) for i in range(size)]


def near_pieces(panel, size):
    cols = panel.shape[1]
    if size != 4:
        held = [(0, panel)]
        bit = 1
        while bit < size:
            held = held + [(rel ^ bit, lax.ppermute(x, "col", flips(size, bit))) for rel, x in held]
            bit *= 2
        return [(0, 0, panel)], [(rel, 0, x) for rel, x in held[1:]]
    near = lax.ppermute(panel, "col", flips(4, 1))
    half = cols // 2
    low, high = panel[:, :half], panel[:, half:]
    far_low = lax.ppermute(low, "col", flips(4, 3))
    far_high = lax.ppermute(high, "col", flips(4, 3))
    return [(0, 0, low), (0, half, high)], [(1, 0, near), (3, 0, far_low), (3, half, far_high)]


def opposite_pieces(near, far_low):
    half = far_low.shape[1]
    cross_low = lax.ppermute(far_low, "col", flips(4, 1))
    cross_high = lax.ppermute(near[:, half:], "col", flips(4, 3))
    return [(2, 0, cross_low), (2, half, cross_high)]


def make_plan(arrival, nb, width_bits, rows_ref, cols_ref, counts_ref, plan_ref):
    slots = rows_ref.shape[-1]
    nb_bits, span_bits, row_bits = width_bits
    part = nb // STREAMS
    me_row, me_col = lax.axis_index("row"), lax.axis_index("col")
    global_rows, global_cols = rows_ref[0], cols_ref[0]
    owner = (global_rows >> span_bits) ^ me_row
    inner = global_rows & (nb - 1)
    rest = owner >> 1
    mirrored = jnp.zeros_like(rest)
    for b in range(row_bits - 1):
        mirrored = mirrored | (((rest >> b) & 1) << (row_bits - 2 - b))
    stream = inner >> (part.bit_length() - 1)
    route = jnp.where(stream & 1 == 1, rest, mirrored)
    target = ((stream << (row_bits - 1)) + route) * part + (inner & (part - 1))
    rel_col = ((global_cols & ((1 << span_bits) - 1)) >> nb_bits) ^ me_col
    phase, place = jnp.zeros_like(rel_col), jnp.zeros_like(rel_col)
    shards = [(p, rel) for p, rels in enumerate(arrival) for rel in rels]
    for at, (p, rel) in enumerate(shards):
        phase = jnp.where(rel_col == rel, p, phase)
        place = jnp.where(rel_col == rel, at, place)
    tile = (place << nb_bits) + (global_cols & (nb - 1))
    keep = len(arrival) + 1
    slot = lax.broadcasted_iota(jnp.int32, (1, slots), 1)
    key = jnp.where(owner & 1 == 0, jnp.where(phase == 0, keep - 1, keep), phase)
    key = jnp.where(slot < counts_ref[0, 0], key, keep + 1)
    key_order = key * slots + slot
    wide = plan_ref.shape[1]
    fill = jnp.zeros((1, wide - slots), jnp.int32)
    both = jnp.concatenate(
        [jnp.concatenate([x, fill], axis=1) for x in (key_order, slot, target, tile)] + [jnp.zeros((4, wide), jnp.int32)],
        axis=0,
    )
    columns = jnp.transpose(both.astype(jnp.float32))[:slots].astype(jnp.int32)
    rank = jnp.sum((key_order < columns[:, 0:1]).astype(jnp.int32), axis=1, keepdims=True)
    hit = rank == lax.broadcasted_iota(jnp.int32, (slots, wide), 1)
    for i in range(3):
        plan_ref[i : i + 1, :] = jnp.sum(jnp.where(hit, columns[:, i + 1 : i + 2], 0), axis=0, keepdims=True)
    lane = lax.broadcasted_iota(jnp.int32, (1, wide), 1)
    bounds = jnp.zeros((1, wide), jnp.int32)
    for k in range(1, keep + 2):
        bounds = jnp.where(lane == k, jnp.sum((key < k).astype(jnp.int32), axis=1, keepdims=True), bounds)
    plan_ref[3:4, :] = bounds
    plan_ref[4:8, :] = jnp.zeros((4, wide), jnp.int32)


def add_products(plan_ref, bucket, tiles, base, blocks_ref, acc_ref, ready=None, done=0):
    begin, end = plan_ref[3, bucket], plan_ref[3, bucket + 1]
    blank = tiles.shape[0] - 1

    def step(group, start, g, carry):
        first = start + g * group
        if ready is not None:
            carry = ready(plan_ref[0, jnp.minimum(first + group, end) - 1], carry)
        parts, targets = [], []
        for u in range(group):
            at = first + u
            real = jnp.minimum(at, end - 1)
            left = tiles[jnp.where(at < end, plan_ref[2, real] - base, blank)]
            parts.append(
                lax.dot_general(
                    left, blocks_ref[plan_ref[0, real]], (((1,), (1,)), ((), ())), preferred_element_type=jnp.float32
                )
            )
            targets.append(plan_ref[1, real])
        for part, target in zip(parts, targets):
            acc_ref[target] += part
        return carry

    half = GROUP // 2
    whole = (end - begin + half - 1) // GROUP
    done = lax.fori_loop(0, whole, functools.partial(step, GROUP, begin), done)
    rest = (jnp.maximum(end - begin - whole * GROUP, 0) + half - 1) // half
    return lax.fori_loop(0, rest, functools.partial(step, half, begin + whole * GROUP), done)


def fill_tiles(where, piece_refs, tiles):
    width = tiles.shape[2]
    for first, ref in zip(where, piece_refs):
        for i in range(ref.shape[1] // width):
            tiles[first + i] = ref[:, i * width : (i + 1) * width]
    tiles[tiles.shape[0] - 1] = jnp.zeros(tiles.shape[1:], tiles.dtype)


def first_kernel(where, arrival, nb, width_bits, rows_ref, cols_ref, counts_ref, *refs):
    piece_refs = refs[: len(where)]
    blocks_ref, acc_ref, keep_ref, store_ref, plan_ref, plan, tiles, rows, cols, sems, plan_sems = refs[len(where) :]
    chunks = sems.shape[0]
    size = blocks_ref.shape[0] // chunks

    def chunk(c):
        part = pl.ds(c * size, size)
        return pltpu.make_async_copy(blocks_ref.at[part], store_ref.at[part], sems.at[c])

    indices = [pltpu.make_async_copy(a, b, plan_sems.at[i]) for i, (a, b) in enumerate(((rows_ref, rows), (cols_ref, cols)))]
    for copy in indices:
        copy.start()
    for copy in indices:
        copy.wait()
    for c in range(chunks):
        chunk(c).start()

    def wait(c, carry):
        chunk(c).wait()
        return carry

    def ready(slot, done):
        need = slot // size + 1
        lax.fori_loop(done, need, wait, 0)
        return jnp.maximum(done, need)

    fill_tiles(where, piece_refs, tiles)
    acc_ref[...] = jnp.zeros_like(acc_ref)
    keep_ref[...] = jnp.zeros_like(keep_ref)
    make_plan(arrival, nb, width_bits, rows, cols, counts_ref, plan_ref)
    to_scalar = pltpu.make_async_copy(plan_ref, plan, plan_sems.at[2])
    to_scalar.start()
    to_scalar.wait()
    done = add_products(plan, 0, tiles, 0, store_ref, acc_ref, ready)
    done = add_products(plan, len(arrival), tiles, 0, store_ref, keep_ref, ready, done)
    lax.fori_loop(done, chunks, wait, 0)


def multiply_first(block_rows, block_cols, counts, arrival, pieces, blocks, nb, rows, grid_rows, grid_cols):
    slots, width, _ = blocks.shape
    panel_cols = pieces[0][1].shape[0]
    bits = (nb.bit_length() - 1, (nb * grid_cols).bit_length() - 1, grid_rows.bit_length() - 1)
    vmem = pl.BlockSpec(memory_space=pltpu.VMEM)
    hbm = pl.BlockSpec(memory_space=pltpu.HBM)
    plan_shape = (8, -(-slots // 128) * 128)
    return pl.pallas_call(
        functools.partial(first_kernel, [first for first, _ in pieces], arrival, nb, bits),
        out_shape=(
            jax.ShapeDtypeStruct((rows, panel_cols, width), jnp.float32),
            jax.ShapeDtypeStruct((rows, panel_cols, width), jnp.float32),
            jax.ShapeDtypeStruct(blocks.shape, blocks.dtype),
            jax.ShapeDtypeStruct(plan_shape, jnp.int32),
        ),
        in_specs=[hbm, hbm, pl.BlockSpec(memory_space=pltpu.SMEM)] + [vmem] * len(pieces) + [hbm],
        out_specs=(vmem, vmem, vmem, vmem),
        scratch_shapes=[
            pltpu.SMEM(plan_shape, jnp.int32),
            pltpu.VMEM((nb + 1, panel_cols, width), pieces[0][1].dtype),
            pltpu.VMEM(block_rows.shape, jnp.int32),
            pltpu.VMEM(block_cols.shape, jnp.int32),
            pltpu.SemaphoreType.DMA((CHUNKS,)),
            pltpu.SemaphoreType.DMA((3,)),
        ],
        compiler_params=pltpu.CompilerParams(vmem_limit_bytes=VMEM_LIMIT),
        cost_estimate=pl.CostEstimate(
            flops=slots // 8 * panel_cols * width * width * 2, bytes_accessed=2 * blocks.size, transcendentals=0
        ),
        name="multiply_first",
    )(
        pltpu.with_memory_space_constraint(block_rows, pltpu.HBM),
        pltpu.with_memory_space_constraint(block_cols, pltpu.HBM),
        counts,
        *[x for _, x in pieces],
        pltpu.with_memory_space_constraint(blocks, pltpu.HBM),
    )


def next_kernel(where, bucket, base, plan_ref, *refs):
    piece_refs = refs[: len(where)]
    blocks_ref = refs[len(where)]
    acc_ref, tiles = refs[-2:]
    fill_tiles(where, piece_refs, tiles)
    if len(refs) == len(where) + 3:
        acc_ref[...] = jnp.zeros_like(acc_ref)
    add_products(plan_ref, bucket, tiles, base, blocks_ref, acc_ref)


def multiply_next(plan, bucket, pieces, blocks, rows, total=None):
    panel_cols = pieces[0][1].shape[0]
    slots, width, _ = blocks.shape
    base = min(first for first, _ in pieces)
    tiles = sum(x.shape[1] for _, x in pieces) // width
    vmem = pl.BlockSpec(memory_space=pltpu.VMEM)
    operands = [plan, *[x for _, x in pieces], blocks] + ([] if total is None else [total])
    share = slots * len(pieces) // 16
    return pl.pallas_call(
        functools.partial(next_kernel, [first - base for first, _ in pieces], bucket, base),
        out_shape=jax.ShapeDtypeStruct((rows, panel_cols, width), jnp.float32),
        in_specs=[pl.BlockSpec(memory_space=pltpu.SMEM)] + [vmem] * (len(operands) - 1),
        out_specs=vmem,
        scratch_shapes=[pltpu.VMEM((tiles + 1, panel_cols, width), pieces[0][1].dtype)],
        input_output_aliases={} if total is None else {len(operands) - 1: 0},
        compiler_params=pltpu.CompilerParams(vmem_limit_bytes=VMEM_LIMIT),
        cost_estimate=pl.CostEstimate(
            flops=share * panel_cols * width * width * 2, bytes_accessed=share * width * width * 2, transcendentals=0
        ),
        name="multiply_next",
    )(*operands)


def encode(rows, out_ref):
    shape = rows[0].shape
    lane = lax.broadcasted_iota(jnp.int32, shape, 1)
    scales = jnp.zeros(shape, jnp.int32)
    for i, row in enumerate(rows):
        top = jnp.max(jnp.abs(row), axis=1, keepdims=True)
        code = jnp.ceil(jnp.log2(jnp.maximum(top, 2.0**-100)) * 128.0) + 1.0
        out_ref[i] = jnp.round(row * jnp.exp2(15.0 - code / 128.0)).astype(jnp.int32).astype(jnp.int16)
        scales = jnp.where(lane == i, jnp.broadcast_to(code.astype(jnp.int32), shape), scales)
    out_ref[len(rows)] = scales.astype(jnp.int16)


def decode(ref):
    n, shape = ref.shape[0] - 1, ref.shape[1:]
    steps = jnp.exp2(ref[n].astype(jnp.int32).astype(jnp.float32) / 128.0 - 15.0)
    return lambda i: ref[i].astype(jnp.int32).astype(jnp.float32) * jnp.broadcast_to(steps[:, i : i + 1], shape)


def reader(ref):
    return decode(ref) if ref.dtype == jnp.int16 else lambda i: ref[i]


def split_kernel(a_ref, b_ref, *outs):
    got = reader(b_ref)
    at = 0
    for keep_ref, send_ref in zip(outs[0::2], outs[1::2]):
        n = keep_ref.shape[0]
        for i in range(n):
            keep_ref[i] = a_ref[at + i] + got(at + i)
        encode([a_ref[at + n + i] + got(at + n + i) for i in range(n)], send_ref)
        at += 2 * n


def add_and_split(a, b, pairs):
    n, rest = a.shape[0] // (2 * pairs), a.shape[1:]
    vmem = pl.BlockSpec(memory_space=pltpu.VMEM)
    return pl.pallas_call(
        split_kernel,
        out_shape=[jax.ShapeDtypeStruct((n,) + rest, a.dtype), jax.ShapeDtypeStruct((n + 1,) + rest, jnp.int16)] * pairs,
        in_specs=[vmem, vmem],
        out_specs=[vmem] * (2 * pairs),
        compiler_params=pltpu.CompilerParams(vmem_limit_bytes=VMEM_LIMIT),
        name="add_and_split",
    )(a, b)


def far_kernel(a_ref, b_ref, *outs):
    got = reader(b_ref)
    n = outs[0].shape[0] - 1
    for k, out in enumerate(outs):
        encode([a_ref[(4 * k + 3) * n + j] + got((4 * k + 3) * n + j) for j in range(n)], out)


def near_kernel(a_ref, b_ref, *outs):
    got = reader(b_ref)
    n = outs[0].shape[0]
    for k in range(len(outs) // 3):
        for i, out in enumerate(outs[3 * k : 3 * k + 3]):
            at = (4 * k + i) * n
            rows = [a_ref[at + j] + got(at + j) for j in range(n)]
            if i < 2:
                for j in range(n):
                    out[j] = rows[j]
            else:
                encode(rows, out)


def spread(a, b, streams):
    n, rest = a.shape[0] // (4 * streams), a.shape[1:]
    vmem = pl.BlockSpec(memory_space=pltpu.VMEM)
    plain, coded = jax.ShapeDtypeStruct((n,) + rest, a.dtype), jax.ShapeDtypeStruct((n + 1,) + rest, jnp.int16)

    def call(kernel, shapes, name):
        return pl.pallas_call(
            kernel,
            out_shape=shapes,
            in_specs=[vmem, vmem],
            out_specs=[vmem] * len(shapes),
            compiler_params=pltpu.CompilerParams(vmem_limit_bytes=VMEM_LIMIT),
            name=name,
        )(a, b)

    far = call(far_kernel, [coded] * streams, "spread_far")
    near = call(near_kernel, [plain, plain, coded] * streams, "spread_near")
    return [(*near[3 * k : 3 * k + 3], far[k]) for k in range(streams)]


def relay_kernel(a_ref, b_ref, out_ref):
    got = reader(b_ref)
    encode([a_ref[i] + got(i) for i in range(a_ref.shape[0])], out_ref)


def relay(a, b):
    vmem = pl.BlockSpec(memory_space=pltpu.VMEM)
    return pl.pallas_call(
        relay_kernel,
        out_shape=jax.ShapeDtypeStruct(b.shape, b.dtype),
        in_specs=[vmem, vmem],
        out_specs=vmem,
        compiler_params=pltpu.CompilerParams(vmem_limit_bytes=VMEM_LIMIT),
        name="relay",
    )(a, b)


def split3(x):
    high = x.astype(jnp.bfloat16)
    rest = x - high.astype(jnp.float32)
    middle = rest.astype(jnp.bfloat16)
    return high, middle, (rest - middle.astype(jnp.float32)).astype(jnp.bfloat16)


def gram_kernel(first, *refs):
    a, b_ref, c_ref = refs[:3]
    stack_ref, gram_ref = refs[-2:]
    b, c = reader(b_ref), reader(c_ref)
    s = a.shape[1]
    products = jnp.zeros((3 * s, 3 * s), jnp.float32) if first else refs[3][...]
    for at in range(0, a.shape[0], 2):
        stacks = []
        for i in (at, at + 1):
            stack = jnp.concatenate(split3(a[i] + b(i) + c(i)), axis=0)
            stack_ref[i] = stack
            stacks.append(stack)
        both = jnp.concatenate(stacks, axis=1)
        products += lax.dot_general(both, both, (((1,), (1,)), ((), ())), preferred_element_type=jnp.float32)
    if len(gram_ref.shape) == 2:
        gram_ref[...] = products
        return
    gram = jnp.zeros((s, s), jnp.float32)
    for i in range(3):
        for j in range(3 - i):
            gram += products[i * s : (i + 1) * s, j * s : (j + 1) * s]
    height = gram_ref.shape[1]
    packed = jnp.concatenate([gram[i : i + height] for i in range(0, s, height)], axis=1)
    for i in range(gram_ref.shape[0]):
        gram_ref[i] = packed


def gram_of(terms, copies):
    vmem = pl.BlockSpec(memory_space=pltpu.VMEM)
    stacks, products = [], []
    for k, term in enumerate(terms):
        n, s, width = term[0].shape
        last = k == len(terms) - 1
        shape = (copies, s * s // width, width) if last else (3 * s, 3 * s)
        stack, total = pl.pallas_call(
            functools.partial(gram_kernel, k == 0),
            out_shape=(jax.ShapeDtypeStruct((n, 3 * s, width), jnp.bfloat16), jax.ShapeDtypeStruct(shape, jnp.float32)),
            in_specs=[vmem] * (3 + len(products)),
            out_specs=[vmem, vmem],
            compiler_params=pltpu.CompilerParams(vmem_limit_bytes=VMEM_LIMIT),
            name="gram",
        )(*term, *products)
        stacks.append(stack)
        products = [total]
    return stacks, products[0]


def factor_kernel(total_rows, grams_ref, *refs):
    stack_refs, (basis_ref, factor_ref) = refs[:-2], refs[-2:]
    s = factor_ref.shape[0]
    width = grams_ref.shape[2]
    packed = jnp.sum(grams_ref[...], axis=0) / total_rows
    gram = jnp.concatenate([packed[:, i : i + s] for i in range(0, width, s)], axis=0)
    ri = lax.broadcasted_iota(jnp.int32, (s, width), 0)
    ci = lax.broadcasted_iota(jnp.int32, (s, width), 1)
    unit = jnp.where(ri == ci, 1.0, 0.0).astype(jnp.float32)[:, :s]
    work = jnp.concatenate([gram, unit, jnp.zeros((s, width - 2 * s), jnp.float32)], axis=1)
    pivots = jnp.ones((s, width), jnp.float32)
    flat = lambda x: jnp.broadcast_to(x, (8, width))
    tall = lambda x: jnp.concatenate([x] * (s // 8), axis=0)
    for j in range(0, s, PIVOTS):
        rows = [flat(work[j + p : j + p + 1, :]) for p in range(PIVOTS)]
        columns = [jnp.broadcast_to(work[:, j + p : j + p + 1], (s, width)) for p in range(PIVOTS)]
        entry = [[flat(work[j + p : j + p + 1, j + q : j + q + 1]) for q in range(PIVOTS)] for p in range(PIVOTS)]
        units = []
        for p in range(PIVOTS):
            inverse = 1.0 / entry[p][p]
            units.append(rows[p] * inverse)
            ratio = [entry[p][q] * inverse for q in range(PIVOTS)]
            for q in range(p + 1, PIVOTS):
                rows[q] = rows[q] - entry[p][q] * units[p]
                columns[q] = columns[q] - columns[p] * tall(ratio[q])
                for t in range(q, PIVOTS):
                    entry[q][t] = entry[q][t] - entry[p][q] * ratio[t]
        reduced = work
        for p in range(PIVOTS):
            reduced = reduced - columns[p] * tall(units[p])
        work = jnp.where(ri >= j + PIVOTS, reduced, work)
        for p in range(PIVOTS):
            work = jnp.where(ri == j + p, tall(rows[p]), work)
            pivots = jnp.where(ri == j + p, tall(entry[p][p]), pivots)
    work = work * lax.rsqrt(pivots)
    factor_ref[...] = jnp.where(ci >= ri, work, 0.0)[:, :s]
    high, middle, low = split3(work[:, s : 2 * s])
    left = jnp.concatenate([high, high, high, middle, middle, low], axis=1)
    at = 0
    for stack_ref in stack_refs:
        for i in range(0, stack_ref.shape[0], 2):
            both = jnp.concatenate([stack_ref[i], stack_ref[i + 1]], axis=1)
            right = jnp.concatenate([both, both[: 2 * s], both[:s]], axis=0)
            basis_ref[:, at : at + 2 * width] = jnp.dot(left, right, preferred_element_type=jnp.float32).astype(
                basis_ref.dtype
            )
            at += 2 * width


def finish(grams, stacks, total_rows):
    vmem = pl.BlockSpec(memory_space=pltpu.VMEM)
    _, rows3, width = stacks[0].shape
    n, s = sum(stack.shape[0] for stack in stacks), rows3 // 3
    return pl.pallas_call(
        functools.partial(factor_kernel, total_rows),
        out_shape=(
            jax.ShapeDtypeStruct((s, n * width), jnp.bfloat16),
            jax.ShapeDtypeStruct((s, s), jnp.float32),
        ),
        in_specs=[vmem] * (1 + len(stacks)),
        out_specs=[vmem, vmem],
        compiler_params=pltpu.CompilerParams(vmem_limit_bytes=VMEM_LIMIT),
        name="finish",
    )(grams, *stacks)


def on_device(blocks, block_rows, block_cols, counts, panel):
    width = blocks.shape[-1]
    nb = panel.shape[1] // width
    grid_rows = lax.axis_size("row")
    grid_cols = lax.axis_size("col")
    bits = grid_rows.bit_length() - 1
    rows = grid_rows * nb // 2

    own, near = near_pieces(panel, grid_cols)
    arrival = [[0], list(dict.fromkeys(rel for rel, _, _ in near))] + ([[2]] if grid_cols == 4 else [])
    order = [rel for rels in arrival for rel in rels]
    number = lambda pieces: [(order.index(rel) * nb + column // width, x) for rel, column, x in pieces]

    send, keep, store, plan = multiply_first(
        block_rows, block_cols, counts, arrival, number(own), blocks[0, 0], nb, rows, grid_rows, grid_cols
    )
    phases = [own, near]
    if grid_cols == 4:
        first, second, send = lax.optimization_barrier((near[0][2], near[1][2], send))
        phases.append(opposite_pieces(first, second))
    phases = [number(pieces) for pieces in phases]
    send = multiply_next(plan, 1, phases[1], store, rows, total=send)
    if grid_cols == 4:
        send = multiply_next(plan, 2, phases[2], store, rows, total=send)
    got = lax.ppermute(send, "row", flips(grid_rows, 1))
    rest = [piece for pieces in phases[1:] for piece in pieces]
    keep = multiply_next(plan, len(phases) + 1, rest, store, rows, total=keep)

    move = lambda x, i, stage: lax.ppermute(x, "row", flips(grid_rows, 1 << (bits - stage if i % 2 else stage)))
    if bits > 3:
        parts = add_and_split(keep, got, STREAMS)
        streams = [(parts[2 * i], move(parts[2 * i + 1], i, 1)) for i in range(STREAMS)]
        for stage in range(2, bits - 2):
            parts = [add_and_split(kept, x, 1) for kept, x in streams]
            streams = [(kept, move(x, i, stage)) for i, (kept, x) in enumerate(parts)]
        streams = [spread(kept, x, 1)[0] for kept, x in streams]
    else:
        streams = spread(keep, got, STREAMS)
    far = [move(stream[3], i, bits - 2) for i, stream in enumerate(streams)]
    near = [move(stream[2], i, bits - 2) for i, stream in enumerate(streams)]
    last = [move(relay(stream[1], x), i, bits - 1) for i, (stream, x) in enumerate(zip(streams, far))]
    streams = [(stream[0], x, y) for stream, x, y in zip(streams, near, last)]

    devices = grid_rows * grid_cols
    stacks, grams = gram_of(streams, devices)
    grams = lax.all_to_all(grams, ("row", "col"), 0, 0, tiled=True)
    return finish(grams, stacks, nb * width * devices)


def solution(mesh):
    in_specs = (
        P("row", "col", None, None, None),
        P("row", "col", None),
        P("row", "col", None),
        P("row", "col"),
        P(None, ("row", "col")),
    )
    out_specs = (P(None, ("row", "col")), P())
    return jax.shard_map(
        on_device, mesh=mesh, in_specs=in_specs, out_specs=out_specs, check_vma=False
    )
```

```python
import functools

import jax
import jax.numpy as jnp
from jax import lax
from jax.experimental import pallas as pl
from jax.experimental.pallas import tpu as pltpu
from jax.sharding import PartitionSpec as P

GROUP = 32
STREAMS = 2
VMEM_LIMIT = 16 << 20
CHUNKS = 10
PIVOTS = 8


def flips(size, mask):
    return [(i, i ^ mask) for i in range(size)]


def near_pieces(panel, size):
    if size != 4:
        held = [(0, panel)]
        bit = 1
        while bit < size:
            held = held + [(rel ^ bit, lax.ppermute(x, "col", flips(size, bit))) for rel, x in held]
            bit *= 2
        return [(0, 0, panel)], [(rel, 0, x) for rel, x in held[1:]]
    far = lax.ppermute(panel, "col", flips(4, 3))
    near = lax.ppermute(panel, "col", flips(4, 1))
    return [(0, 0, panel)], [(3, 0, far), (1, 0, near)]


def make_plan(arrival, nb, width_bits, rows_ref, cols_ref, counts_ref, plan_ref):
    slots = rows_ref.shape[-1]
    nb_bits, span_bits, row_bits = width_bits
    part = nb // STREAMS
    me_row, me_col = lax.axis_index("row"), lax.axis_index("col")
    global_rows, global_cols = rows_ref[0], cols_ref[0]
    owner = (global_rows >> span_bits) ^ me_row
    inner = global_rows & (nb - 1)
    rest = owner >> 1
    mirrored = jnp.zeros_like(rest)
    for b in range(row_bits - 1):
        mirrored = mirrored | (((rest >> b) & 1) << (row_bits - 2 - b))
    stream = inner >> (part.bit_length() - 1)
    route = jnp.where(stream & 1 == 1, rest, mirrored)
    target = ((stream << (row_bits - 1)) + route) * part + (inner & (part - 1))
    rel_col = ((global_cols & ((1 << span_bits) - 1)) >> nb_bits) ^ me_col
    phase, place = jnp.zeros_like(rel_col), jnp.zeros_like(rel_col)
    shards = [(p, rel) for p, rels in enumerate(arrival) for rel in rels]
    for at, (p, rel) in enumerate(shards):
        phase = jnp.where(rel_col == rel, p, phase)
        place = jnp.where(rel_col == rel, at, place)
    tile = (place << nb_bits) + (global_cols & (nb - 1))
    keep = len(arrival) + 1
    slot = lax.broadcasted_iota(jnp.int32, (1, slots), 1)
    key = jnp.where(owner & 1 == 0, jnp.where(phase == 0, keep - 1, keep), phase)
    key = jnp.where(slot < counts_ref[0, 0], key, keep + 1)
    key_order = key * slots + slot
    wide = plan_ref.shape[1]
    fill = jnp.zeros((1, wide - slots), jnp.int32)
    both = jnp.concatenate(
        [jnp.concatenate([x, fill], axis=1) for x in (key_order, slot, target, tile)] + [jnp.zeros((4, wide), jnp.int32)],
        axis=0,
    )
    columns = jnp.transpose(both.astype(jnp.float32))[:slots].astype(jnp.int32)
    rank = jnp.sum((key_order < columns[:, 0:1]).astype(jnp.int32), axis=1, keepdims=True)
    hit = rank == lax.broadcasted_iota(jnp.int32, (slots, wide), 1)
    for i in range(3):
        plan_ref[i : i + 1, :] = jnp.sum(jnp.where(hit, columns[:, i + 1 : i + 2], 0), axis=0, keepdims=True)
    lane = lax.broadcasted_iota(jnp.int32, (1, wide), 1)
    bounds = jnp.zeros((1, wide), jnp.int32)
    for k in range(1, keep + 2):
        bounds = jnp.where(lane == k, jnp.sum((key < k).astype(jnp.int32), axis=1, keepdims=True), bounds)
    plan_ref[3:4, :] = bounds
    plan_ref[4:8, :] = jnp.zeros((4, wide), jnp.int32)


def add_products(plan_ref, bucket, tiles, base, blocks_ref, acc_ref, ready=None, done=0):
    begin, end = plan_ref[3, bucket], plan_ref[3, bucket + 1]
    blank = tiles.shape[0] - 1

    def step(group, start, g, carry):
        first = start + g * group
        if ready is not None:
            carry = ready(plan_ref[0, jnp.minimum(first + group, end) - 1], carry)
        parts, targets = [], []
        for u in range(group):
            at = first + u
            real = jnp.minimum(at, end - 1)
            left = tiles[jnp.where(at < end, plan_ref[2, real] - base, blank)]
            parts.append(
                lax.dot_general(
                    left, blocks_ref[plan_ref[0, real]], (((1,), (1,)), ((), ())), preferred_element_type=jnp.float32
                )
            )
            targets.append(plan_ref[1, real])
        for part, target in zip(parts, targets):
            acc_ref[target] += part
        return carry

    half = GROUP // 2
    whole = (end - begin + half - 1) // GROUP
    done = lax.fori_loop(0, whole, functools.partial(step, GROUP, begin), done)
    rest = (jnp.maximum(end - begin - whole * GROUP, 0) + half - 1) // half
    return lax.fori_loop(0, rest, functools.partial(step, half, begin + whole * GROUP), done)


def fill_tiles(where, piece_refs, tiles):
    width = tiles.shape[2]
    for first, ref in zip(where, piece_refs):
        for i in range(ref.shape[1] // width):
            tiles[first + i] = ref[:, i * width : (i + 1) * width]
    tiles[tiles.shape[0] - 1] = jnp.zeros(tiles.shape[1:], tiles.dtype)


def first_kernel(arrival, nb, width_bits, rows_ref, cols_ref, counts_ref, panel_ref, blocks_ref, *refs):
    acc_ref, keep_ref, store_ref, plan_ref, plan, tiles, rows, cols, panel, sems, plan_sems = refs
    chunks = sems.shape[0]
    size = blocks_ref.shape[0] // chunks

    def chunk(c):
        part = pl.ds(c * size, size)
        return pltpu.make_async_copy(blocks_ref.at[part], store_ref.at[part], sems.at[c])

    indices = [pltpu.make_async_copy(a, b, plan_sems.at[i]) for i, (a, b) in enumerate(((rows_ref, rows), (cols_ref, cols), (panel_ref, panel)))]
    for copy in indices:
        copy.start()
    for copy in indices:
        copy.wait()
    for c in range(chunks):
        chunk(c).start()

    def wait(c, carry):
        chunk(c).wait()
        return carry

    def ready(slot, done):
        need = slot // size + 1
        lax.fori_loop(done, need, wait, 0)
        return jnp.maximum(done, need)

    fill_tiles([0], [panel], tiles)
    acc_ref[...] = jnp.zeros_like(acc_ref)
    keep_ref[...] = jnp.zeros_like(keep_ref)
    make_plan(arrival, nb, width_bits, rows, cols, counts_ref, plan_ref)
    to_scalar = pltpu.make_async_copy(plan_ref, plan, plan_sems.at[3])
    to_scalar.start()
    to_scalar.wait()
    done = add_products(plan, 0, tiles, 0, store_ref, acc_ref, ready)
    done = add_products(plan, len(arrival), tiles, 0, store_ref, keep_ref, ready, done)
    lax.fori_loop(done, chunks, wait, 0)


def multiply_first(block_rows, block_cols, counts, arrival, panel, blocks, nb, rows, grid_rows, grid_cols):
    slots, width, _ = blocks.shape
    panel_cols = panel.shape[0]
    bits = (nb.bit_length() - 1, (nb * grid_cols).bit_length() - 1, grid_rows.bit_length() - 1)
    vmem = pl.BlockSpec(memory_space=pltpu.VMEM)
    hbm = pl.BlockSpec(memory_space=pltpu.HBM)
    plan_shape = (8, -(-slots // 128) * 128)
    return pl.pallas_call(
        functools.partial(first_kernel, arrival, nb, bits),
        out_shape=(
            jax.ShapeDtypeStruct((rows, panel_cols, width), jnp.float32),
            jax.ShapeDtypeStruct((rows, panel_cols, width), jnp.float32),
            jax.ShapeDtypeStruct(blocks.shape, blocks.dtype),
            jax.ShapeDtypeStruct(plan_shape, jnp.int32),
        ),
        in_specs=[hbm, hbm, pl.BlockSpec(memory_space=pltpu.SMEM), hbm, hbm],
        out_specs=(vmem, vmem, vmem, vmem),
        scratch_shapes=[
            pltpu.SMEM(plan_shape, jnp.int32),
            pltpu.VMEM((nb + 1, panel_cols, width), panel.dtype),
            pltpu.VMEM(block_rows.shape, jnp.int32),
            pltpu.VMEM(block_cols.shape, jnp.int32),
            pltpu.VMEM(panel.shape, panel.dtype),
            pltpu.SemaphoreType.DMA((CHUNKS,)),
            pltpu.SemaphoreType.DMA((4,)),
        ],
        compiler_params=pltpu.CompilerParams(vmem_limit_bytes=VMEM_LIMIT),
        cost_estimate=pl.CostEstimate(
            flops=slots // 8 * panel_cols * width * width * 2, bytes_accessed=2 * blocks.size, transcendentals=0
        ),
        name="multiply_first",
    )(
        pltpu.with_memory_space_constraint(block_rows, pltpu.HBM),
        pltpu.with_memory_space_constraint(block_cols, pltpu.HBM),
        counts,
        pltpu.with_memory_space_constraint(panel, pltpu.HBM),
        pltpu.with_memory_space_constraint(blocks, pltpu.HBM),
    )


def next_kernel(where, bucket, base, plan_ref, *refs):
    piece_refs = refs[: len(where)]
    blocks_ref = refs[len(where)]
    acc_ref, tiles = refs[-2:]
    fill_tiles(where, piece_refs, tiles)
    if len(refs) == len(where) + 3:
        acc_ref[...] = jnp.zeros_like(acc_ref)
    add_products(plan_ref, bucket, tiles, base, blocks_ref, acc_ref)


def multiply_next(plan, bucket, pieces, blocks, rows, total=None):
    panel_cols = pieces[0][1].shape[0]
    slots, width, _ = blocks.shape
    base = min(first for first, _ in pieces)
    tiles = sum(x.shape[1] for _, x in pieces) // width
    vmem = pl.BlockSpec(memory_space=pltpu.VMEM)
    operands = [plan, *[x for _, x in pieces], blocks] + ([] if total is None else [total])
    share = slots * len(pieces) // 16
    return pl.pallas_call(
        functools.partial(next_kernel, [first - base for first, _ in pieces], bucket, base),
        out_shape=jax.ShapeDtypeStruct((rows, panel_cols, width), jnp.float32),
        in_specs=[pl.BlockSpec(memory_space=pltpu.SMEM)] + [vmem] * (len(operands) - 1),
        out_specs=vmem,
        scratch_shapes=[pltpu.VMEM((tiles + 1, panel_cols, width), pieces[0][1].dtype)],
        input_output_aliases={} if total is None else {len(operands) - 1: 0},
        compiler_params=pltpu.CompilerParams(vmem_limit_bytes=VMEM_LIMIT),
        cost_estimate=pl.CostEstimate(
            flops=share * panel_cols * width * width * 2, bytes_accessed=share * width * width * 2, transcendentals=0
        ),
        name="multiply_next",
    )(*operands)


def encode(rows, out_ref):
    shape = rows[0].shape
    lane = lax.broadcasted_iota(jnp.int32, shape, 1)
    scales = jnp.zeros(shape, jnp.int32)
    for i, row in enumerate(rows):
        top = jnp.max(jnp.abs(row), axis=1, keepdims=True)
        code = jnp.ceil(jnp.log2(jnp.maximum(top, 2.0**-100)) * 128.0) + 1.0
        out_ref[i] = jnp.round(row * jnp.exp2(15.0 - code / 128.0)).astype(jnp.int32).astype(jnp.int16)
        scales = jnp.where(lane == i, jnp.broadcast_to(code.astype(jnp.int32), shape), scales)
    out_ref[len(rows)] = scales.astype(jnp.int16)


def decode(ref):
    n, shape = ref.shape[0] - 1, ref.shape[1:]
    steps = jnp.exp2(ref[n].astype(jnp.int32).astype(jnp.float32) / 128.0 - 15.0)
    return lambda i: ref[i].astype(jnp.int32).astype(jnp.float32) * jnp.broadcast_to(steps[:, i : i + 1], shape)


def reader(ref):
    return decode(ref) if ref.dtype == jnp.int16 else lambda i: ref[i]


def split_kernel(a_ref, b_ref, *outs):
    got = reader(b_ref)
    at = 0
    for keep_ref, send_ref in zip(outs[0::2], outs[1::2]):
        n = keep_ref.shape[0]
        for i in range(n):
            keep_ref[i] = a_ref[at + i] + got(at + i)
        encode([a_ref[at + n + i] + got(at + n + i) for i in range(n)], send_ref)
        at += 2 * n


def add_and_split(a, b, pairs):
    n, rest = a.shape[0] // (2 * pairs), a.shape[1:]
    vmem = pl.BlockSpec(memory_space=pltpu.VMEM)
    return pl.pallas_call(
        split_kernel,
        out_shape=[jax.ShapeDtypeStruct((n,) + rest, a.dtype), jax.ShapeDtypeStruct((n + 1,) + rest, jnp.int16)] * pairs,
        in_specs=[vmem, vmem],
        out_specs=[vmem] * (2 * pairs),
        compiler_params=pltpu.CompilerParams(vmem_limit_bytes=VMEM_LIMIT),
        name="add_and_split",
    )(a, b)


def far_kernel(a_ref, b_ref, *outs):
    got = reader(b_ref)
    n = outs[0].shape[0] - 1
    for k, out in enumerate(outs):
        encode([a_ref[(4 * k + 3) * n + j] + got((4 * k + 3) * n + j) for j in range(n)], out)


def near_kernel(a_ref, b_ref, *outs):
    got = reader(b_ref)
    n = outs[0].shape[0]
    for k in range(len(outs) // 3):
        for i, out in enumerate(outs[3 * k : 3 * k + 3]):
            at = (4 * k + i) * n
            rows = [a_ref[at + j] + got(at + j) for j in range(n)]
            if i < 2:
                for j in range(n):
                    out[j] = rows[j]
            else:
                encode(rows, out)


def spread(a, b, streams):
    n, rest = a.shape[0] // (4 * streams), a.shape[1:]
    vmem = pl.BlockSpec(memory_space=pltpu.VMEM)
    plain, coded = jax.ShapeDtypeStruct((n,) + rest, a.dtype), jax.ShapeDtypeStruct((n + 1,) + rest, jnp.int16)

    def call(kernel, shapes, name):
        return pl.pallas_call(
            kernel,
            out_shape=shapes,
            in_specs=[vmem, vmem],
            out_specs=[vmem] * len(shapes),
            compiler_params=pltpu.CompilerParams(vmem_limit_bytes=VMEM_LIMIT),
            name=name,
        )(a, b)

    far = call(far_kernel, [coded] * streams, "spread_far")
    near = call(near_kernel, [plain, plain, coded] * streams, "spread_near")
    return [(*near[3 * k : 3 * k + 3], far[k]) for k in range(streams)]


def relay_kernel(a_ref, b_ref, out_ref):
    got = reader(b_ref)
    encode([a_ref[i] + got(i) for i in range(a_ref.shape[0])], out_ref)


def relay(a, b):
    vmem = pl.BlockSpec(memory_space=pltpu.VMEM)
    return pl.pallas_call(
        relay_kernel,
        out_shape=jax.ShapeDtypeStruct(b.shape, b.dtype),
        in_specs=[vmem, vmem],
        out_specs=vmem,
        compiler_params=pltpu.CompilerParams(vmem_limit_bytes=VMEM_LIMIT),
        name="relay",
    )(a, b)


def split3(x):
    high = x.astype(jnp.bfloat16)
    rest = x - high.astype(jnp.float32)
    middle = rest.astype(jnp.bfloat16)
    return high, middle, (rest - middle.astype(jnp.float32)).astype(jnp.bfloat16)


def gram_kernel(first, *refs):
    a, b_ref, c_ref = refs[:3]
    stack_ref, gram_ref = refs[-2:]
    b, c = reader(b_ref), reader(c_ref)
    s = a.shape[1]
    products = jnp.zeros((3 * s, 3 * s), jnp.float32) if first else refs[3][...]
    for at in range(0, a.shape[0], 2):
        stacks = []
        for i in (at, at + 1):
            stack = jnp.concatenate(split3(a[i] + b(i) + c(i)), axis=0)
            stack_ref[i] = stack
            stacks.append(stack)
        both = jnp.concatenate(stacks, axis=1)
        products += lax.dot_general(both, both, (((1,), (1,)), ((), ())), preferred_element_type=jnp.float32)
    if len(gram_ref.shape) == 2:
        gram_ref[...] = products
        return
    gram = jnp.zeros((s, s), jnp.float32)
    for i in range(3):
        for j in range(3 - i):
            gram += products[i * s : (i + 1) * s, j * s : (j + 1) * s]
    height = gram_ref.shape[1]
    packed = jnp.concatenate([gram[i : i + height] for i in range(0, s, height)], axis=1)
    for i in range(gram_ref.shape[0]):
        gram_ref[i] = packed


def gram_of(terms, copies):
    vmem = pl.BlockSpec(memory_space=pltpu.VMEM)
    stacks, products = [], []
    for k, term in enumerate(terms):
        n, s, width = term[0].shape
        last = k == len(terms) - 1
        shape = (copies, s * s // width, width) if last else (3 * s, 3 * s)
        stack, total = pl.pallas_call(
            functools.partial(gram_kernel, k == 0),
            out_shape=(jax.ShapeDtypeStruct((n, 3 * s, width), jnp.bfloat16), jax.ShapeDtypeStruct(shape, jnp.float32)),
            in_specs=[vmem] * (3 + len(products)),
            out_specs=[vmem, vmem],
            compiler_params=pltpu.CompilerParams(vmem_limit_bytes=VMEM_LIMIT),
            name="gram",
        )(*term, *products)
        stacks.append(stack)
        products = [total]
    return stacks, products[0]


def factor_kernel(total_rows, grams_ref, *refs):
    stack_refs, (basis_ref, factor_ref) = refs[:-2], refs[-2:]
    s = factor_ref.shape[0]
    width = grams_ref.shape[2]
    packed = jnp.sum(grams_ref[...], axis=0) / total_rows
    gram = jnp.concatenate([packed[:, i : i + s] for i in range(0, width, s)], axis=0)
    ri = lax.broadcasted_iota(jnp.int32, (s, width), 0)
    ci = lax.broadcasted_iota(jnp.int32, (s, width), 1)
    unit = jnp.where(ri == ci, 1.0, 0.0).astype(jnp.float32)[:, :s]
    work = jnp.concatenate([gram, unit, jnp.zeros((s, width - 2 * s), jnp.float32)], axis=1)
    pivots = jnp.ones((s, width), jnp.float32)
    flat = lambda x: jnp.broadcast_to(x, (8, width))
    tall = lambda x: jnp.concatenate([x] * (s // 8), axis=0)
    for j in range(0, s, PIVOTS):
        rows = [flat(work[j + p : j + p + 1, :]) for p in range(PIVOTS)]
        columns = [jnp.broadcast_to(work[:, j + p : j + p + 1], (s, width)) for p in range(PIVOTS)]
        entry = [[flat(work[j + p : j + p + 1, j + q : j + q + 1]) for q in range(PIVOTS)] for p in range(PIVOTS)]
        units = []
        for p in range(PIVOTS):
            inverse = 1.0 / entry[p][p]
            units.append(rows[p] * inverse)
            ratio = [entry[p][q] * inverse for q in range(PIVOTS)]
            for q in range(p + 1, PIVOTS):
                rows[q] = rows[q] - entry[p][q] * units[p]
                columns[q] = columns[q] - columns[p] * tall(ratio[q])
                for t in range(q, PIVOTS):
                    entry[q][t] = entry[q][t] - entry[p][q] * ratio[t]
        reduced = work
        for p in range(PIVOTS):
            reduced = reduced - columns[p] * tall(units[p])
        work = jnp.where(ri >= j + PIVOTS, reduced, work)
        for p in range(PIVOTS):
            work = jnp.where(ri == j + p, tall(rows[p]), work)
            pivots = jnp.where(ri == j + p, tall(entry[p][p]), pivots)
    work = work * lax.rsqrt(pivots)
    factor_ref[...] = jnp.where(ci >= ri, work, 0.0)[:, :s]
    high, middle, low = split3(work[:, s : 2 * s])
    left = jnp.concatenate([high, high, high, middle, middle, low], axis=1)
    at = 0
    for stack_ref in stack_refs:
        for i in range(0, stack_ref.shape[0], 2):
            both = jnp.concatenate([stack_ref[i], stack_ref[i + 1]], axis=1)
            right = jnp.concatenate([both, both[: 2 * s], both[:s]], axis=0)
            basis_ref[:, at : at + 2 * width] = jnp.dot(left, right, preferred_element_type=jnp.float32).astype(
                basis_ref.dtype
            )
            at += 2 * width


def finish(grams, stacks, total_rows):
    vmem = pl.BlockSpec(memory_space=pltpu.VMEM)
    _, rows3, width = stacks[0].shape
    n, s = sum(stack.shape[0] for stack in stacks), rows3 // 3
    return pl.pallas_call(
        functools.partial(factor_kernel, total_rows),
        out_shape=(
            jax.ShapeDtypeStruct((s, n * width), jnp.bfloat16),
            jax.ShapeDtypeStruct((s, s), jnp.float32),
        ),
        in_specs=[vmem] * (1 + len(stacks)),
        out_specs=[vmem, vmem],
        compiler_params=pltpu.CompilerParams(vmem_limit_bytes=VMEM_LIMIT),
        name="finish",
    )(grams, *stacks)


def on_device(blocks, block_rows, block_cols, counts, panel):
    width = blocks.shape[-1]
    nb = panel.shape[1] // width
    grid_rows = lax.axis_size("row")
    grid_cols = lax.axis_size("col")
    bits = grid_rows.bit_length() - 1
    rows = grid_rows * nb // 2

    own, near = near_pieces(panel, grid_cols)
    arrival = [[0], list(dict.fromkeys(rel for rel, _, _ in near))] + ([[2]] if grid_cols == 4 else [])
    order = [rel for rels in arrival for rel in rels]
    number = lambda pieces: [(order.index(rel) * nb + column // width, x) for rel, column, x in pieces]

    send, keep, store, plan = multiply_first(
        block_rows, block_cols, counts, arrival, panel, blocks[0, 0], nb, rows, grid_rows, grid_cols
    )
    phases = [own, near]
    if grid_cols == 4:
        far, send = lax.optimization_barrier((near[0][2], send))
        phases.append([(2, 0, lax.ppermute(far, "col", flips(4, 1)))])
    phases = [number(pieces) for pieces in phases]
    send = multiply_next(plan, 1, phases[1], store, rows, total=send)
    if grid_cols == 4:
        send = multiply_next(plan, 2, phases[2], store, rows, total=send)
    got = lax.ppermute(send, "row", flips(grid_rows, 1))
    rest = [piece for pieces in phases[1:] for piece in pieces]
    keep = multiply_next(plan, len(phases) + 1, rest, store, rows, total=keep)

    move = lambda x, i, stage: lax.ppermute(x, "row", flips(grid_rows, 1 << (bits - stage if i % 2 else stage)))
    if bits > 3:
        parts = add_and_split(keep, got, STREAMS)
        streams = [(parts[2 * i], move(parts[2 * i + 1], i, 1)) for i in range(STREAMS)]
        for stage in range(2, bits - 2):
            parts = [add_and_split(kept, x, 1) for kept, x in streams]
            streams = [(kept, move(x, i, stage)) for i, (kept, x) in enumerate(parts)]
        streams = [spread(kept, x, 1)[0] for kept, x in streams]
    else:
        streams = spread(keep, got, STREAMS)
    far = [move(stream[3], i, bits - 2) for i, stream in enumerate(streams)]
    near = [move(stream[2], i, bits - 2) for i, stream in enumerate(streams)]
    last = [move(relay(stream[1], x), i, bits - 1) for i, (stream, x) in enumerate(zip(streams, far))]
    streams = [(stream[0], x, y) for stream, x, y in zip(streams, near, last)]

    devices = grid_rows * grid_cols
    stacks, grams = gram_of(streams, devices)
    grams = lax.all_to_all(grams, ("row", "col"), 0, 0, tiled=True)
    return finish(grams, stacks, nb * width * devices)


def solution(mesh):
    in_specs = (
        P("row", "col", None, None, None),
        P("row", "col", None),
        P("row", "col", None),
        P("row", "col"),
        P(None, ("row", "col")),
    )
    out_specs = (P(None, ("row", "col")), P())
    return jax.shard_map(
        on_device, mesh=mesh, in_specs=in_specs, out_specs=out_specs, check_vma=False
    )
```

```python
import functools

import jax
import jax.numpy as jnp
from jax import lax
from jax.experimental import pallas as pl
from jax.experimental.pallas import tpu as pltpu
from jax.sharding import PartitionSpec as P

GROUP = 32
STREAMS = 2
VMEM_LIMIT = 16 << 20
CHUNKS = 10
PIVOTS = 8


def flips(size, mask):
    return [(i, i ^ mask) for i in range(size)]


def near_pieces(panel, size):
    if size != 4:
        held = [(0, panel)]
        bit = 1
        while bit < size:
            held = held + [(rel ^ bit, lax.ppermute(x, "col", flips(size, bit))) for rel, x in held]
            bit *= 2
        return [(0, 0, panel)], [(rel, 0, x) for rel, x in held[1:]]
    far = lax.ppermute(panel, "col", flips(4, 3))
    near = lax.ppermute(panel, "col", flips(4, 1))
    return [(0, 0, panel)], [(3, 0, far), (1, 0, near)]


def make_plan(arrival, nb, width_bits, rows_ref, cols_ref, counts_ref, plan_ref):
    slots = rows_ref.shape[-1]
    nb_bits, span_bits, row_bits = width_bits
    part = nb // STREAMS
    me_row, me_col = lax.axis_index("row"), lax.axis_index("col")
    global_rows, global_cols = rows_ref[0], cols_ref[0]
    owner = (global_rows >> span_bits) ^ me_row
    inner = global_rows & (nb - 1)
    rest = owner >> 1
    mirrored = jnp.zeros_like(rest)
    for b in range(row_bits - 1):
        mirrored = mirrored | (((rest >> b) & 1) << (row_bits - 2 - b))
    stream = inner >> (part.bit_length() - 1)
    route = jnp.where(stream & 1 == 1, rest, mirrored)
    target = ((stream << (row_bits - 1)) + route) * part + (inner & (part - 1))
    rel_col = ((global_cols & ((1 << span_bits) - 1)) >> nb_bits) ^ me_col
    phase, place = jnp.zeros_like(rel_col), jnp.zeros_like(rel_col)
    shards = [(p, rel) for p, rels in enumerate(arrival) for rel in rels]
    for at, (p, rel) in enumerate(shards):
        phase = jnp.where(rel_col == rel, p, phase)
        place = jnp.where(rel_col == rel, at, place)
    tile = (place << nb_bits) + (global_cols & (nb - 1))
    phases = len(arrival)
    slot = lax.broadcasted_iota(jnp.int32, (1, slots), 1)
    key = jnp.where(owner & 1 == 0, phase + phases, phase)
    key = jnp.where(slot < counts_ref[0, 0], key, 2 * phases)
    key_order = key * slots + slot
    wide = plan_ref.shape[1]
    fill = jnp.zeros((1, wide - slots), jnp.int32)
    both = jnp.concatenate(
        [jnp.concatenate([x, fill], axis=1) for x in (key_order, slot, target, tile)] + [jnp.zeros((4, wide), jnp.int32)],
        axis=0,
    )
    columns = jnp.transpose(both.astype(jnp.float32))[:slots].astype(jnp.int32)
    rank = jnp.sum((key_order < columns[:, 0:1]).astype(jnp.int32), axis=1, keepdims=True)
    hit = rank == lax.broadcasted_iota(jnp.int32, (slots, wide), 1)
    for i in range(3):
        plan_ref[i : i + 1, :] = jnp.sum(jnp.where(hit, columns[:, i + 1 : i + 2], 0), axis=0, keepdims=True)
    lane = lax.broadcasted_iota(jnp.int32, (1, wide), 1)
    bounds = jnp.zeros((1, wide), jnp.int32)
    for k in range(1, 2 * phases + 1):
        bounds = jnp.where(lane == k, jnp.sum((key < k).astype(jnp.int32), axis=1, keepdims=True), bounds)
    plan_ref[3:4, :] = bounds
    plan_ref[4:8, :] = jnp.zeros((4, wide), jnp.int32)


def add_products(plan_ref, bucket, tiles, base, blocks_ref, acc_ref, ready=None, done=0):
    begin, end = plan_ref[3, bucket], plan_ref[3, bucket + 1]
    blank = tiles.shape[0] - 1

    def step(group, start, g, carry):
        first = start + g * group
        if ready is not None:
            carry = ready(plan_ref[0, jnp.minimum(first + group, end) - 1], carry)
        parts, targets = [], []
        for u in range(group):
            at = first + u
            real = jnp.minimum(at, end - 1)
            left = tiles[jnp.where(at < end, plan_ref[2, real] - base, blank)]
            parts.append(
                lax.dot_general(
                    left, blocks_ref[plan_ref[0, real]], (((1,), (1,)), ((), ())), preferred_element_type=jnp.float32
                )
            )
            targets.append(plan_ref[1, real])
        for part, target in zip(parts, targets):
            acc_ref[target] += part
        return carry

    half = GROUP // 2
    whole = (end - begin + half - 1) // GROUP
    done = lax.fori_loop(0, whole, functools.partial(step, GROUP, begin), done)
    rest = (jnp.maximum(end - begin - whole * GROUP, 0) + half - 1) // half
    return lax.fori_loop(0, rest, functools.partial(step, half, begin + whole * GROUP), done)


def fill_tiles(where, piece_refs, tiles):
    width = tiles.shape[2]
    for first, ref in zip(where, piece_refs):
        for i in range(ref.shape[1] // width):
            tiles[first + i] = ref[:, i * width : (i + 1) * width]
    tiles[tiles.shape[0] - 1] = jnp.zeros(tiles.shape[1:], tiles.dtype)


def first_kernel(arrival, nb, width_bits, rows_ref, cols_ref, counts_ref, panel_ref, blocks_ref, *refs):
    acc_ref, keep_ref, store_ref, plan_ref, plan, tiles, rows, cols, panel, sems, plan_sems = refs
    chunks = sems.shape[0]
    size = blocks_ref.shape[0] // chunks

    def chunk(c):
        part = pl.ds(c * size, size)
        return pltpu.make_async_copy(blocks_ref.at[part], store_ref.at[part], sems.at[c])

    indices = [pltpu.make_async_copy(a, b, plan_sems.at[i]) for i, (a, b) in enumerate(((rows_ref, rows), (cols_ref, cols), (panel_ref, panel)))]
    for copy in indices:
        copy.start()
    for copy in indices:
        copy.wait()
    for c in range(chunks):
        chunk(c).start()

    def wait(c, carry):
        chunk(c).wait()
        return carry

    def ready(slot, done):
        need = slot // size + 1
        lax.fori_loop(done, need, wait, 0)
        return jnp.maximum(done, need)

    fill_tiles([0], [panel], tiles)
    acc_ref[...] = jnp.zeros_like(acc_ref)
    keep_ref[...] = jnp.zeros_like(keep_ref)
    make_plan(arrival, nb, width_bits, rows, cols, counts_ref, plan_ref)
    to_scalar = pltpu.make_async_copy(plan_ref, plan, plan_sems.at[3])
    to_scalar.start()
    to_scalar.wait()
    done = add_products(plan, 0, tiles, 0, store_ref, acc_ref, ready)
    done = add_products(plan, len(arrival), tiles, 0, store_ref, keep_ref, ready, done)
    lax.fori_loop(done, chunks, wait, 0)


def multiply_first(block_rows, block_cols, counts, arrival, panel, blocks, nb, rows, grid_rows, grid_cols):
    slots, width, _ = blocks.shape
    panel_cols = panel.shape[0]
    bits = (nb.bit_length() - 1, (nb * grid_cols).bit_length() - 1, grid_rows.bit_length() - 1)
    vmem = pl.BlockSpec(memory_space=pltpu.VMEM)
    hbm = pl.BlockSpec(memory_space=pltpu.HBM)
    plan_shape = (8, -(-slots // 128) * 128)
    return pl.pallas_call(
        functools.partial(first_kernel, arrival, nb, bits),
        out_shape=(
            jax.ShapeDtypeStruct((rows, panel_cols, width), jnp.float32),
            jax.ShapeDtypeStruct((rows, panel_cols, width), jnp.float32),
            jax.ShapeDtypeStruct(blocks.shape, blocks.dtype),
            jax.ShapeDtypeStruct(plan_shape, jnp.int32),
        ),
        in_specs=[hbm, hbm, pl.BlockSpec(memory_space=pltpu.SMEM), hbm, hbm],
        out_specs=(vmem, vmem, vmem, vmem),
        scratch_shapes=[
            pltpu.SMEM(plan_shape, jnp.int32),
            pltpu.VMEM((nb + 1, panel_cols, width), panel.dtype),
            pltpu.VMEM(block_rows.shape, jnp.int32),
            pltpu.VMEM(block_cols.shape, jnp.int32),
            pltpu.VMEM(panel.shape, panel.dtype),
            pltpu.SemaphoreType.DMA((CHUNKS,)),
            pltpu.SemaphoreType.DMA((4,)),
        ],
        compiler_params=pltpu.CompilerParams(vmem_limit_bytes=VMEM_LIMIT),
        cost_estimate=pl.CostEstimate(
            flops=slots // 8 * panel_cols * width * width * 2, bytes_accessed=2 * blocks.size, transcendentals=0
        ),
        name="multiply_first",
    )(
        pltpu.with_memory_space_constraint(block_rows, pltpu.HBM),
        pltpu.with_memory_space_constraint(block_cols, pltpu.HBM),
        counts,
        pltpu.with_memory_space_constraint(panel, pltpu.HBM),
        pltpu.with_memory_space_constraint(blocks, pltpu.HBM),
    )


def next_kernel(where, bucket, base, plan_ref, *refs):
    piece_refs = refs[: len(where)]
    blocks_ref = refs[len(where)]
    acc_ref, tiles = refs[-2:]
    fill_tiles(where, piece_refs, tiles)
    add_products(plan_ref, bucket, tiles, base, blocks_ref, acc_ref)


def multiply_next(plan, bucket, pieces, blocks, total):
    panel_cols = pieces[0][1].shape[0]
    slots, width, _ = blocks.shape
    base = min(first for first, _ in pieces)
    tiles = sum(x.shape[1] for _, x in pieces) // width
    vmem = pl.BlockSpec(memory_space=pltpu.VMEM)
    operands = [plan, *[x for _, x in pieces], blocks, total]
    share = slots * len(pieces) // 16
    return pl.pallas_call(
        functools.partial(next_kernel, [first - base for first, _ in pieces], bucket, base),
        out_shape=jax.ShapeDtypeStruct(total.shape, total.dtype),
        in_specs=[pl.BlockSpec(memory_space=pltpu.SMEM)] + [vmem] * (len(operands) - 1),
        out_specs=vmem,
        scratch_shapes=[pltpu.VMEM((tiles + 1, panel_cols, width), pieces[0][1].dtype)],
        input_output_aliases={len(operands) - 1: 0},
        compiler_params=pltpu.CompilerParams(vmem_limit_bytes=VMEM_LIMIT),
        cost_estimate=pl.CostEstimate(
            flops=share * panel_cols * width * width * 2, bytes_accessed=share * width * width * 2, transcendentals=0
        ),
        name="multiply_next",
    )(*operands)


def encode(rows, out_ref):
    shape = rows[0].shape
    lane = lax.broadcasted_iota(jnp.int32, shape, 1)
    scales = jnp.zeros(shape, jnp.int32)
    for i, row in enumerate(rows):
        top = jnp.max(jnp.abs(row), axis=1, keepdims=True)
        code = jnp.ceil(jnp.log2(jnp.maximum(top, 2.0**-100)) * 128.0) + 1.0
        out_ref[i] = jnp.round(row * jnp.exp2(15.0 - code / 128.0)).astype(jnp.int32).astype(jnp.int16)
        scales = jnp.where(lane == i, jnp.broadcast_to(code.astype(jnp.int32), shape), scales)
    out_ref[len(rows)] = scales.astype(jnp.int16)


def decode(ref):
    n, shape = ref.shape[0] - 1, ref.shape[1:]
    steps = jnp.exp2(ref[n].astype(jnp.int32).astype(jnp.float32) / 128.0 - 15.0)
    return lambda i: ref[i].astype(jnp.int32).astype(jnp.float32) * jnp.broadcast_to(steps[:, i : i + 1], shape)


def reader(ref):
    return decode(ref) if ref.dtype == jnp.int16 else lambda i: ref[i]


def split_kernel(a_ref, b_ref, *outs):
    got = reader(b_ref)
    at = 0
    for keep_ref, send_ref in zip(outs[0::2], outs[1::2]):
        n = keep_ref.shape[0]
        for i in range(n):
            keep_ref[i] = a_ref[at + i] + got(at + i)
        encode([a_ref[at + n + i] + got(at + n + i) for i in range(n)], send_ref)
        at += 2 * n


def add_and_split(a, b, pairs):
    n, rest = a.shape[0] // (2 * pairs), a.shape[1:]
    vmem = pl.BlockSpec(memory_space=pltpu.VMEM)
    return pl.pallas_call(
        split_kernel,
        out_shape=[jax.ShapeDtypeStruct((n,) + rest, a.dtype), jax.ShapeDtypeStruct((n + 1,) + rest, jnp.int16)] * pairs,
        in_specs=[vmem, vmem],
        out_specs=[vmem] * (2 * pairs),
        compiler_params=pltpu.CompilerParams(vmem_limit_bytes=VMEM_LIMIT),
        name="add_and_split",
    )(a, b)


def far_kernel(a_ref, b_ref, *outs):
    got = reader(b_ref)
    n = outs[0].shape[0] - 1
    for k, out in enumerate(outs):
        encode([a_ref[(4 * k + 3) * n + j] + got((4 * k + 3) * n + j) for j in range(n)], out)


def near_kernel(a_ref, b_ref, *outs):
    got = reader(b_ref)
    n = outs[0].shape[0]
    for k in range(len(outs) // 3):
        for i, out in enumerate(outs[3 * k : 3 * k + 3]):
            at = (4 * k + i) * n
            rows = [a_ref[at + j] + got(at + j) for j in range(n)]
            if i < 2:
                for j in range(n):
                    out[j] = rows[j]
            else:
                encode(rows, out)


def spread(a, b, streams):
    n, rest = a.shape[0] // (4 * streams), a.shape[1:]
    vmem = pl.BlockSpec(memory_space=pltpu.VMEM)
    plain, coded = jax.ShapeDtypeStruct((n,) + rest, a.dtype), jax.ShapeDtypeStruct((n + 1,) + rest, jnp.int16)

    def call(kernel, shapes, name):
        return pl.pallas_call(
            kernel,
            out_shape=shapes,
            in_specs=[vmem, vmem],
            out_specs=[vmem] * len(shapes),
            compiler_params=pltpu.CompilerParams(vmem_limit_bytes=VMEM_LIMIT),
            name=name,
        )(a, b)

    far = call(far_kernel, [coded] * streams, "spread_far")
    near = call(near_kernel, [plain, plain, coded] * streams, "spread_near")
    return [(*near[3 * k : 3 * k + 3], far[k]) for k in range(streams)]


def relay_kernel(a_ref, b_ref, out_ref):
    got = reader(b_ref)
    encode([a_ref[i] + got(i) for i in range(a_ref.shape[0])], out_ref)


def relay(a, b):
    vmem = pl.BlockSpec(memory_space=pltpu.VMEM)
    return pl.pallas_call(
        relay_kernel,
        out_shape=jax.ShapeDtypeStruct(b.shape, b.dtype),
        in_specs=[vmem, vmem],
        out_specs=vmem,
        compiler_params=pltpu.CompilerParams(vmem_limit_bytes=VMEM_LIMIT),
        name="relay",
    )(a, b)


def split3(x):
    high = x.astype(jnp.bfloat16)
    rest = x - high.astype(jnp.float32)
    middle = rest.astype(jnp.bfloat16)
    return high, middle, (rest - middle.astype(jnp.float32)).astype(jnp.bfloat16)


def gram_kernel(first, *refs):
    a, b_ref, c_ref = refs[:3]
    stack_ref, gram_ref = refs[-2:]
    b, c = reader(b_ref), reader(c_ref)
    s = a.shape[1]
    products = jnp.zeros((3 * s, 3 * s), jnp.float32) if first else refs[3][...]
    for at in range(0, a.shape[0], 2):
        stacks = []
        for i in (at, at + 1):
            stack = jnp.concatenate(split3(a[i] + b(i) + c(i)), axis=0)
            stack_ref[i] = stack
            stacks.append(stack)
        both = jnp.concatenate(stacks, axis=1)
        products += lax.dot_general(both, both, (((1,), (1,)), ((), ())), preferred_element_type=jnp.float32)
    if len(gram_ref.shape) == 2:
        gram_ref[...] = products
        return
    gram = jnp.zeros((s, s), jnp.float32)
    for i in range(3):
        for j in range(3 - i):
            gram += products[i * s : (i + 1) * s, j * s : (j + 1) * s]
    height = gram_ref.shape[1]
    packed = jnp.concatenate([gram[i : i + height] for i in range(0, s, height)], axis=1)
    for i in range(gram_ref.shape[0]):
        gram_ref[i] = packed


def gram_of(terms, copies):
    vmem = pl.BlockSpec(memory_space=pltpu.VMEM)
    stacks, products = [], []
    for k, term in enumerate(terms):
        n, s, width = term[0].shape
        last = k == len(terms) - 1
        shape = (copies, s * s // width, width) if last else (3 * s, 3 * s)
        stack, total = pl.pallas_call(
            functools.partial(gram_kernel, k == 0),
            out_shape=(jax.ShapeDtypeStruct((n, 3 * s, width), jnp.bfloat16), jax.ShapeDtypeStruct(shape, jnp.float32)),
            in_specs=[vmem] * (3 + len(products)),
            out_specs=[vmem, vmem],
            compiler_params=pltpu.CompilerParams(vmem_limit_bytes=VMEM_LIMIT),
            name="gram",
        )(*term, *products)
        stacks.append(stack)
        products = [total]
    return stacks, products[0]


def factor_kernel(total_rows, grams_ref, *refs):
    stack_refs, (basis_ref, factor_ref) = refs[:-2], refs[-2:]
    s = factor_ref.shape[0]
    width = grams_ref.shape[2]
    packed = jnp.sum(grams_ref[...], axis=0) / total_rows
    gram = jnp.concatenate([packed[:, i : i + s] for i in range(0, width, s)], axis=0)
    ri = lax.broadcasted_iota(jnp.int32, (s, width), 0)
    ci = lax.broadcasted_iota(jnp.int32, (s, width), 1)
    unit = jnp.where(ri == ci, 1.0, 0.0).astype(jnp.float32)[:, :s]
    work = jnp.concatenate([gram, unit, jnp.zeros((s, width - 2 * s), jnp.float32)], axis=1)
    pivots = jnp.ones((s, width), jnp.float32)
    flat = lambda x: jnp.broadcast_to(x, (8, width))
    tall = lambda x: jnp.concatenate([x] * (s // 8), axis=0)
    for j in range(0, s, PIVOTS):
        rows = [flat(work[j + p : j + p + 1, :]) for p in range(PIVOTS)]
        columns = [jnp.broadcast_to(work[:, j + p : j + p + 1], (s, width)) for p in range(PIVOTS)]
        entry = [[flat(work[j + p : j + p + 1, j + q : j + q + 1]) for q in range(PIVOTS)] for p in range(PIVOTS)]
        units = []
        for p in range(PIVOTS):
            inverse = 1.0 / entry[p][p]
            units.append(rows[p] * inverse)
            ratio = [entry[p][q] * inverse for q in range(PIVOTS)]
            for q in range(p + 1, PIVOTS):
                rows[q] = rows[q] - entry[p][q] * units[p]
                columns[q] = columns[q] - columns[p] * tall(ratio[q])
                for t in range(q, PIVOTS):
                    entry[q][t] = entry[q][t] - entry[p][q] * ratio[t]
        reduced = work
        for p in range(PIVOTS):
            reduced = reduced - columns[p] * tall(units[p])
        work = jnp.where(ri >= j + PIVOTS, reduced, work)
        for p in range(PIVOTS):
            work = jnp.where(ri == j + p, tall(rows[p]), work)
            pivots = jnp.where(ri == j + p, tall(entry[p][p]), pivots)
    work = work * lax.rsqrt(pivots)
    factor_ref[...] = jnp.where(ci >= ri, work, 0.0)[:, :s]
    high, middle, low = split3(work[:, s : 2 * s])
    left = jnp.concatenate([high, high, high, middle, middle, low], axis=1)
    at = 0
    for stack_ref in stack_refs:
        for i in range(0, stack_ref.shape[0], 2):
            both = jnp.concatenate([stack_ref[i], stack_ref[i + 1]], axis=1)
            right = jnp.concatenate([both, both[: 2 * s], both[:s]], axis=0)
            basis_ref[:, at : at + 2 * width] = jnp.dot(left, right, preferred_element_type=jnp.float32).astype(
                basis_ref.dtype
            )
            at += 2 * width


def finish(grams, stacks, total_rows):
    vmem = pl.BlockSpec(memory_space=pltpu.VMEM)
    _, rows3, width = stacks[0].shape
    n, s = sum(stack.shape[0] for stack in stacks), rows3 // 3
    return pl.pallas_call(
        functools.partial(factor_kernel, total_rows),
        out_shape=(
            jax.ShapeDtypeStruct((s, n * width), jnp.bfloat16),
            jax.ShapeDtypeStruct((s, s), jnp.float32),
        ),
        in_specs=[vmem] * (1 + len(stacks)),
        out_specs=[vmem, vmem],
        compiler_params=pltpu.CompilerParams(vmem_limit_bytes=VMEM_LIMIT),
        name="finish",
    )(grams, *stacks)


def on_device(blocks, block_rows, block_cols, counts, panel):
    width = blocks.shape[-1]
    nb = panel.shape[1] // width
    grid_rows = lax.axis_size("row")
    grid_cols = lax.axis_size("col")
    bits = grid_rows.bit_length() - 1
    rows = grid_rows * nb // 2

    own, near = near_pieces(panel, grid_cols)
    arrival = [[0], list(dict.fromkeys(rel for rel, _, _ in near))] + ([[2]] if grid_cols == 4 else [])
    order = [rel for rels in arrival for rel in rels]
    number = lambda pieces: [(order.index(rel) * nb + column // width, x) for rel, column, x in pieces]

    send, keep, store, plan = multiply_first(
        block_rows, block_cols, counts, arrival, panel, blocks[0, 0], nb, rows, grid_rows, grid_cols
    )
    phases = [own, near]
    if grid_cols == 4:
        far, send = lax.optimization_barrier((near[0][2], send))
        phases.append([(2, 0, lax.ppermute(far, "col", flips(4, 1)))])
    phases = [number(pieces) for pieces in phases]
    count = len(phases)
    if count > 2:
        send = multiply_next(plan, 1, phases[1], store, send)
        keep = multiply_next(plan, count + 1, phases[1], store, keep)
        last, keep = lax.optimization_barrier(([x for _, x in phases[2]], keep))
        phases[2] = [(first, x) for (first, _), x in zip(phases[2], last)]
    send = multiply_next(plan, count - 1, phases[-1], store, send)
    got = lax.ppermute(send, "row", flips(grid_rows, 1))
    keep = multiply_next(plan, 2 * count - 1, phases[-1], store, keep)

    move = lambda x, i, stage: lax.ppermute(x, "row", flips(grid_rows, 1 << (bits - stage if i % 2 else stage)))
    if bits > 3:
        parts = add_and_split(keep, got, STREAMS)
        streams = [(parts[2 * i], move(parts[2 * i + 1], i, 1)) for i in range(STREAMS)]
        for stage in range(2, bits - 2):
            parts = [add_and_split(kept, x, 1) for kept, x in streams]
            streams = [(kept, move(x, i, stage)) for i, (kept, x) in enumerate(parts)]
        streams = [spread(kept, x, 1)[0] for kept, x in streams]
    else:
        streams = spread(keep, got, STREAMS)
    far = [move(stream[3], i, bits - 2) for i, stream in enumerate(streams)]
    near = [move(stream[2], i, bits - 2) for i, stream in enumerate(streams)]
    last = [move(relay(stream[1], x), i, bits - 1) for i, (stream, x) in enumerate(zip(streams, far))]
    streams = [(stream[0], x, y) for stream, x, y in zip(streams, near, last)]

    devices = grid_rows * grid_cols
    stacks, grams = gram_of(streams, devices)
    grams = lax.all_to_all(grams, ("row", "col"), 0, 0, tiled=True)
    return finish(grams, stacks, nb * width * devices)


def solution(mesh):
    in_specs = (
        P("row", "col", None, None, None),
        P("row", "col", None),
        P("row", "col", None),
        P("row", "col"),
        P(None, ("row", "col")),
    )
    out_specs = (P(None, ("row", "col")), P())
    return jax.shard_map(
        on_device, mesh=mesh, in_specs=in_specs, out_specs=out_specs, check_vma=False
    )
```

```python
import functools

import jax
import jax.numpy as jnp
from jax import lax
from jax.experimental import pallas as pl
from jax.experimental.pallas import tpu as pltpu
from jax.sharding import PartitionSpec as P

GROUP = 32
STREAMS = 2
VMEM_LIMIT = 16 << 20
CHUNKS = 10
PIVOTS = 8


def flips(size, mask):
    return [(i, i ^ mask) for i in range(size)]


def near_pieces(panel, size):
    if size != 4:
        held = [(0, panel)]
        bit = 1
        while bit < size:
            held = held + [(rel ^ bit, lax.ppermute(x, "col", flips(size, bit))) for rel, x in held]
            bit *= 2
        return [(0, 0, panel)], [(rel, 0, x) for rel, x in held[1:]]
    far = lax.ppermute(panel, "col", flips(4, 3))
    near = lax.ppermute(panel, "col", flips(4, 1))
    return [(0, 0, panel)], [(3, 0, far), (1, 0, near)]


def make_plan(arrival, nb, width_bits, rows_ref, cols_ref, counts_ref, plan_ref):
    slots = rows_ref.shape[-1]
    nb_bits, span_bits, row_bits = width_bits
    part = nb // STREAMS
    me_row, me_col = lax.axis_index("row"), lax.axis_index("col")
    global_rows, global_cols = rows_ref[0], cols_ref[0]
    owner = (global_rows >> span_bits) ^ me_row
    inner = global_rows & (nb - 1)
    rest = owner >> 1
    mirrored = jnp.zeros_like(rest)
    for b in range(row_bits - 1):
        mirrored = mirrored | (((rest >> b) & 1) << (row_bits - 2 - b))
    stream = inner >> (part.bit_length() - 1)
    route = jnp.where(stream & 1 == 1, rest, mirrored)
    target = ((stream << (row_bits - 1)) + route) * part + (inner & (part - 1))
    rel_col = ((global_cols & ((1 << span_bits) - 1)) >> nb_bits) ^ me_col
    phase, place = jnp.zeros_like(rel_col), jnp.zeros_like(rel_col)
    shards = [(p, rel) for p, rels in enumerate(arrival) for rel in rels]
    for at, (p, rel) in enumerate(shards):
        phase = jnp.where(rel_col == rel, p, phase)
        place = jnp.where(rel_col == rel, at, place)
    tile = (place << nb_bits) + (global_cols & (nb - 1))
    keep = len(arrival) + 1
    slot = lax.broadcasted_iota(jnp.int32, (1, slots), 1)
    key = jnp.where(owner & 1 == 0, jnp.where(phase == 0, keep - 1, keep), phase)
    key = jnp.where(slot < counts_ref[0, 0], key, keep + 1)
    key_order = key * slots + slot
    wide = plan_ref.shape[1]
    fill = jnp.zeros((1, wide - slots), jnp.int32)
    both = jnp.concatenate(
        [jnp.concatenate([x, fill], axis=1) for x in (key_order, slot, target, tile)] + [jnp.zeros((4, wide), jnp.int32)],
        axis=0,
    )
    columns = jnp.transpose(both.astype(jnp.float32))[:slots].astype(jnp.int32)
    rank = jnp.sum((key_order < columns[:, 0:1]).astype(jnp.int32), axis=1, keepdims=True)
    hit = rank == lax.broadcasted_iota(jnp.int32, (slots, wide), 1)
    for i in range(3):
        plan_ref[i : i + 1, :] = jnp.sum(jnp.where(hit, columns[:, i + 1 : i + 2], 0), axis=0, keepdims=True)
    lane = lax.broadcasted_iota(jnp.int32, (1, wide), 1)
    bounds = jnp.zeros((1, wide), jnp.int32)
    for k in range(1, keep + 2):
        bounds = jnp.where(lane == k, jnp.sum((key < k).astype(jnp.int32), axis=1, keepdims=True), bounds)
    plan_ref[3:4, :] = bounds
    plan_ref[4:8, :] = jnp.zeros((4, wide), jnp.int32)


def add_products(plan_ref, bucket, tiles, base, blocks_ref, acc_ref, ready=None, done=0):
    begin, end = plan_ref[3, bucket], plan_ref[3, bucket + 1]
    blank = tiles.shape[0] - 1

    def step(group, start, g, carry):
        first = start + g * group
        if ready is not None:
            carry = ready(plan_ref[0, jnp.minimum(first + group, end) - 1], carry)
        parts, targets = [], []
        for u in range(group):
            at = first + u
            real = jnp.minimum(at, end - 1)
            left = tiles[jnp.where(at < end, plan_ref[2, real] - base, blank)]
            parts.append(
                lax.dot_general(
                    left, blocks_ref[plan_ref[0, real]], (((1,), (1,)), ((), ())), preferred_element_type=jnp.float32
                )
            )
            targets.append(plan_ref[1, real])
        for part, target in zip(parts, targets):
            acc_ref[target] += part
        return carry

    half = GROUP // 2
    whole = (end - begin + half - 1) // GROUP
    done = lax.fori_loop(0, whole, functools.partial(step, GROUP, begin), done)
    rest = (jnp.maximum(end - begin - whole * GROUP, 0) + half - 1) // half
    return lax.fori_loop(0, rest, functools.partial(step, half, begin + whole * GROUP), done)


def fill_tiles(where, piece_refs, tiles):
    width = tiles.shape[2]
    for first, ref in zip(where, piece_refs):
        for i in range(ref.shape[1] // width):
            tiles[first + i] = ref[:, i * width : (i + 1) * width]
    tiles[tiles.shape[0] - 1] = jnp.zeros(tiles.shape[1:], tiles.dtype)


def first_kernel(arrival, nb, width_bits, rows_ref, cols_ref, counts_ref, panel_ref, blocks_ref, *refs):
    acc_ref, keep_ref, store_ref, plan_ref, plan, tiles, rows, cols, panel, sems, plan_sems = refs
    chunks = sems.shape[0]
    size = blocks_ref.shape[0] // chunks

    def chunk(c):
        part = pl.ds(c * size, size)
        return pltpu.make_async_copy(blocks_ref.at[part], store_ref.at[part], sems.at[c])

    indices = [pltpu.make_async_copy(a, b, plan_sems.at[i]) for i, (a, b) in enumerate(((rows_ref, rows), (cols_ref, cols), (panel_ref, panel)))]
    for copy in indices:
        copy.start()
    for copy in indices:
        copy.wait()
    for c in range(chunks):
        chunk(c).start()

    def wait(c, carry):
        chunk(c).wait()
        return carry

    def ready(slot, done):
        need = slot // size + 1
        lax.fori_loop(done, need, wait, 0)
        return jnp.maximum(done, need)

    fill_tiles([0], [panel], tiles)
    acc_ref[...] = jnp.zeros_like(acc_ref)
    keep_ref[...] = jnp.zeros_like(keep_ref)
    make_plan(arrival, nb, width_bits, rows, cols, counts_ref, plan_ref)
    to_scalar = pltpu.make_async_copy(plan_ref, plan, plan_sems.at[3])
    to_scalar.start()
    to_scalar.wait()
    done = add_products(plan, 0, tiles, 0, store_ref, acc_ref, ready)
    done = add_products(plan, len(arrival), tiles, 0, store_ref, keep_ref, ready, done)
    lax.fori_loop(done, chunks, wait, 0)


def multiply_first(block_rows, block_cols, counts, arrival, panel, blocks, nb, rows, grid_rows, grid_cols):
    slots, width, _ = blocks.shape
    panel_cols = panel.shape[0]
    bits = (nb.bit_length() - 1, (nb * grid_cols).bit_length() - 1, grid_rows.bit_length() - 1)
    vmem = pl.BlockSpec(memory_space=pltpu.VMEM)
    hbm = pl.BlockSpec(memory_space=pltpu.HBM)
    plan_shape = (8, -(-slots // 128) * 128)
    return pl.pallas_call(
        functools.partial(first_kernel, arrival, nb, bits),
        out_shape=(
            jax.ShapeDtypeStruct((rows, panel_cols, width), jnp.float32),
            jax.ShapeDtypeStruct((rows, panel_cols, width), jnp.float32),
            jax.ShapeDtypeStruct(blocks.shape, blocks.dtype),
            jax.ShapeDtypeStruct(plan_shape, jnp.int32),
        ),
        in_specs=[hbm, hbm, pl.BlockSpec(memory_space=pltpu.SMEM), hbm, hbm],
        out_specs=(vmem, vmem, vmem, vmem),
        scratch_shapes=[
            pltpu.SMEM(plan_shape, jnp.int32),
            pltpu.VMEM((nb + 1, panel_cols, width), panel.dtype),
            pltpu.VMEM(block_rows.shape, jnp.int32),
            pltpu.VMEM(block_cols.shape, jnp.int32),
            pltpu.VMEM(panel.shape, panel.dtype),
            pltpu.SemaphoreType.DMA((CHUNKS,)),
            pltpu.SemaphoreType.DMA((4,)),
        ],
        compiler_params=pltpu.CompilerParams(vmem_limit_bytes=VMEM_LIMIT),
        cost_estimate=pl.CostEstimate(
            flops=slots // 8 * panel_cols * width * width * 2, bytes_accessed=2 * blocks.size, transcendentals=0
        ),
        name="multiply_first",
    )(
        pltpu.with_memory_space_constraint(block_rows, pltpu.HBM),
        pltpu.with_memory_space_constraint(block_cols, pltpu.HBM),
        counts,
        pltpu.with_memory_space_constraint(panel, pltpu.HBM),
        pltpu.with_memory_space_constraint(blocks, pltpu.HBM),
    )


def next_kernel(where, bucket, base, plan_ref, *refs):
    piece_refs = refs[: len(where)]
    blocks_ref = refs[len(where)]
    acc_ref, tiles = refs[-2:]
    fill_tiles(where, piece_refs, tiles)
    if len(refs) == len(where) + 3:
        acc_ref[...] = jnp.zeros_like(acc_ref)
    add_products(plan_ref, bucket, tiles, base, blocks_ref, acc_ref)


def multiply_next(plan, bucket, pieces, blocks, rows, total=None):
    panel_cols = pieces[0][1].shape[0]
    slots, width, _ = blocks.shape
    base = min(first for first, _ in pieces)
    tiles = sum(x.shape[1] for _, x in pieces) // width
    vmem = pl.BlockSpec(memory_space=pltpu.VMEM)
    operands = [plan, *[x for _, x in pieces], blocks] + ([] if total is None else [total])
    share = slots * len(pieces) // 16
    return pl.pallas_call(
        functools.partial(next_kernel, [first - base for first, _ in pieces], bucket, base),
        out_shape=jax.ShapeDtypeStruct((rows, panel_cols, width), jnp.float32),
        in_specs=[pl.BlockSpec(memory_space=pltpu.SMEM)] + [vmem] * (len(operands) - 1),
        out_specs=vmem,
        scratch_shapes=[pltpu.VMEM((tiles + 1, panel_cols, width), pieces[0][1].dtype)],
        input_output_aliases={} if total is None else {len(operands) - 1: 0},
        compiler_params=pltpu.CompilerParams(vmem_limit_bytes=VMEM_LIMIT),
        cost_estimate=pl.CostEstimate(
            flops=share * panel_cols * width * width * 2, bytes_accessed=share * width * width * 2, transcendentals=0
        ),
        name="multiply_next",
    )(*operands)


def encode(rows, out_ref):
    shape = rows[0].shape
    lane = lax.broadcasted_iota(jnp.int32, shape, 1)
    scales = jnp.zeros(shape, jnp.int32)
    for i, row in enumerate(rows):
        top = jnp.max(jnp.abs(row), axis=1, keepdims=True)
        code = jnp.ceil(jnp.log2(jnp.maximum(top, 2.0**-100)) * 128.0) + 1.0
        out_ref[i] = jnp.round(row * jnp.exp2(15.0 - code / 128.0)).astype(jnp.int32).astype(jnp.int16)
        scales = jnp.where(lane == i, jnp.broadcast_to(code.astype(jnp.int32), shape), scales)
    out_ref[len(rows)] = scales.astype(jnp.int16)


def decode(ref):
    n, shape = ref.shape[0] - 1, ref.shape[1:]
    steps = jnp.exp2(ref[n].astype(jnp.int32).astype(jnp.float32) / 128.0 - 15.0)
    return lambda i: ref[i].astype(jnp.int32).astype(jnp.float32) * jnp.broadcast_to(steps[:, i : i + 1], shape)


def reader(ref):
    return decode(ref) if ref.dtype == jnp.int16 else lambda i: ref[i]


def split_kernel(a_ref, b_ref, *outs):
    got = reader(b_ref)
    at = 0
    for keep_ref, send_ref in zip(outs[0::2], outs[1::2]):
        n = keep_ref.shape[0]
        for i in range(n):
            keep_ref[i] = a_ref[at + i] + got(at + i)
        encode([a_ref[at + n + i] + got(at + n + i) for i in range(n)], send_ref)
        at += 2 * n


def add_and_split(a, b, pairs):
    n, rest = a.shape[0] // (2 * pairs), a.shape[1:]
    vmem = pl.BlockSpec(memory_space=pltpu.VMEM)
    return pl.pallas_call(
        split_kernel,
        out_shape=[jax.ShapeDtypeStruct((n,) + rest, a.dtype), jax.ShapeDtypeStruct((n + 1,) + rest, jnp.int16)] * pairs,
        in_specs=[vmem, vmem],
        out_specs=[vmem] * (2 * pairs),
        compiler_params=pltpu.CompilerParams(vmem_limit_bytes=VMEM_LIMIT),
        name="add_and_split",
    )(a, b)


def far_kernel(a_ref, b_ref, *outs):
    got = reader(b_ref)
    n = outs[0].shape[0] - 1
    for k, out in enumerate(outs):
        encode([a_ref[(4 * k + 3) * n + j] + got((4 * k + 3) * n + j) for j in range(n)], out)


def near_kernel(a_ref, b_ref, *outs):
    got = reader(b_ref)
    n = outs[0].shape[0]
    for k in range(len(outs) // 3):
        for i, out in enumerate(outs[3 * k : 3 * k + 3]):
            at = (4 * k + i) * n
            rows = [a_ref[at + j] + got(at + j) for j in range(n)]
            if i < 2:
                for j in range(n):
                    out[j] = rows[j]
            else:
                encode(rows, out)


def spread(a, b, streams):
    n, rest = a.shape[0] // (4 * streams), a.shape[1:]
    vmem = pl.BlockSpec(memory_space=pltpu.VMEM)
    plain, coded = jax.ShapeDtypeStruct((n,) + rest, a.dtype), jax.ShapeDtypeStruct((n + 1,) + rest, jnp.int16)

    def call(kernel, shapes, name):
        return pl.pallas_call(
            kernel,
            out_shape=shapes,
            in_specs=[vmem, vmem],
            out_specs=[vmem] * len(shapes),
            compiler_params=pltpu.CompilerParams(vmem_limit_bytes=VMEM_LIMIT),
            name=name,
        )(a, b)

    far = call(far_kernel, [coded] * streams, "spread_far")
    near = call(near_kernel, [plain, plain, coded] * streams, "spread_near")
    return [(*near[3 * k : 3 * k + 3], far[k]) for k in range(streams)]


def relay_kernel(a_ref, b_ref, out_ref):
    got = reader(b_ref)
    encode([a_ref[i] + got(i) for i in range(a_ref.shape[0])], out_ref)


def relay(a, b):
    vmem = pl.BlockSpec(memory_space=pltpu.VMEM)
    return pl.pallas_call(
        relay_kernel,
        out_shape=jax.ShapeDtypeStruct(b.shape, b.dtype),
        in_specs=[vmem, vmem],
        out_specs=vmem,
        compiler_params=pltpu.CompilerParams(vmem_limit_bytes=VMEM_LIMIT),
        name="relay",
    )(a, b)


def split3(x):
    high = x.astype(jnp.bfloat16)
    rest = x - high.astype(jnp.float32)
    middle = rest.astype(jnp.bfloat16)
    return high, middle, (rest - middle.astype(jnp.float32)).astype(jnp.bfloat16)


def gram_kernel(first, *refs):
    a, b_ref, c_ref = refs[:3]
    stack_ref, gram_ref = refs[-2:]
    b, c = reader(b_ref), reader(c_ref)
    s = a.shape[1]
    products = jnp.zeros((3 * s, 3 * s), jnp.float32) if first else refs[3][...]
    for at in range(0, a.shape[0], 2):
        stacks = []
        for i in (at, at + 1):
            stack = jnp.concatenate(split3(a[i] + b(i) + c(i)), axis=0)
            stack_ref[i] = stack
            stacks.append(stack)
        both = jnp.concatenate(stacks, axis=1)
        products += lax.dot_general(both, both, (((1,), (1,)), ((), ())), preferred_element_type=jnp.float32)
    if len(gram_ref.shape) == 2:
        gram_ref[...] = products
        return
    gram = jnp.zeros((s, s), jnp.float32)
    for i in range(3):
        for j in range(3 - i):
            gram += products[i * s : (i + 1) * s, j * s : (j + 1) * s]
    height = gram_ref.shape[1]
    packed = jnp.concatenate([gram[i : i + height] for i in range(0, s, height)], axis=1)
    for i in range(gram_ref.shape[0]):
        gram_ref[i] = packed


def gram_of(terms, copies):
    vmem = pl.BlockSpec(memory_space=pltpu.VMEM)
    stacks, products = [], []
    for k, term in enumerate(terms):
        n, s, width = term[0].shape
        last = k == len(terms) - 1
        shape = (copies, s * s // width, width) if last else (3 * s, 3 * s)
        stack, total = pl.pallas_call(
            functools.partial(gram_kernel, k == 0),
            out_shape=(jax.ShapeDtypeStruct((n, 3 * s, width), jnp.bfloat16), jax.ShapeDtypeStruct(shape, jnp.float32)),
            in_specs=[vmem] * (3 + len(products)),
            out_specs=[vmem, vmem],
            compiler_params=pltpu.CompilerParams(vmem_limit_bytes=VMEM_LIMIT),
            name="gram",
        )(*term, *products)
        stacks.append(stack)
        products = [total]
    return stacks, products[0]


def factor_kernel(total_rows, grams_ref, *refs):
    stack_refs, (basis_ref, factor_ref) = refs[:-2], refs[-2:]
    s = factor_ref.shape[0]
    width = grams_ref.shape[2]
    packed = jnp.sum(grams_ref[...], axis=0) / total_rows
    gram = jnp.concatenate([packed[:, i : i + s] for i in range(0, width, s)], axis=0)
    ri = lax.broadcasted_iota(jnp.int32, (s, width), 0)
    ci = lax.broadcasted_iota(jnp.int32, (s, width), 1)
    unit = jnp.where(ri == ci, 1.0, 0.0).astype(jnp.float32)[:, :s]
    work = jnp.concatenate([gram, unit, jnp.zeros((s, width - 2 * s), jnp.float32)], axis=1)
    pivots = jnp.ones((s, width), jnp.float32)
    flat = lambda x: jnp.broadcast_to(x, (8, width))
    tall = lambda x: jnp.concatenate([x] * (s // 8), axis=0)
    for j in range(0, s, PIVOTS):
        rows = [flat(work[j + p : j + p + 1, :]) for p in range(PIVOTS)]
        columns = [jnp.broadcast_to(work[:, j + p : j + p + 1], (s, width)) for p in range(PIVOTS)]
        entry = [[flat(work[j + p : j + p + 1, j + q : j + q + 1]) for q in range(PIVOTS)] for p in range(PIVOTS)]
        units = []
        for p in range(PIVOTS):
            root = lax.rsqrt(entry[p][p])
            units.append(rows[p] * root * root)
            ratio = [entry[p][q] * root * root for q in range(PIVOTS)]
            for q in range(p + 1, PIVOTS):
                rows[q] = rows[q] - entry[p][q] * units[p]
                columns[q] = columns[q] - columns[p] * tall(ratio[q])
                for t in range(q, PIVOTS):
                    entry[q][t] = entry[q][t] - entry[p][q] * ratio[t]
        reduced = work
        for p in range(PIVOTS):
            reduced = reduced - columns[p] * tall(units[p])
        work = jnp.where(ri >= j + PIVOTS, reduced, work)
        for p in range(PIVOTS):
            work = jnp.where(ri == j + p, tall(rows[p]), work)
            pivots = jnp.where(ri == j + p, tall(entry[p][p]), pivots)
    work = work * lax.rsqrt(pivots)
    factor_ref[...] = jnp.where(ci >= ri, work, 0.0)[:, :s]
    high, middle, low = split3(work[:, s : 2 * s])
    left = jnp.concatenate([high, high, high, middle, middle, low], axis=1)
    at = 0
    for stack_ref in stack_refs:
        for i in range(0, stack_ref.shape[0], 2):
            both = jnp.concatenate([stack_ref[i], stack_ref[i + 1]], axis=1)
            right = jnp.concatenate([both, both[: 2 * s], both[:s]], axis=0)
            basis_ref[:, at : at + 2 * width] = jnp.dot(left, right, preferred_element_type=jnp.float32).astype(
                basis_ref.dtype
            )
            at += 2 * width


def finish(grams, stacks, total_rows):
    vmem = pl.BlockSpec(memory_space=pltpu.VMEM)
    _, rows3, width = stacks[0].shape
    n, s = sum(stack.shape[0] for stack in stacks), rows3 // 3
    return pl.pallas_call(
        functools.partial(factor_kernel, total_rows),
        out_shape=(
            jax.ShapeDtypeStruct((s, n * width), jnp.bfloat16),
            jax.ShapeDtypeStruct((s, s), jnp.float32),
        ),
        in_specs=[vmem] * (1 + len(stacks)),
        out_specs=[vmem, vmem],
        compiler_params=pltpu.CompilerParams(vmem_limit_bytes=VMEM_LIMIT),
        name="finish",
    )(grams, *stacks)


def on_device(blocks, block_rows, block_cols, counts, panel):
    width = blocks.shape[-1]
    nb = panel.shape[1] // width
    grid_rows = lax.axis_size("row")
    grid_cols = lax.axis_size("col")
    bits = grid_rows.bit_length() - 1
    rows = grid_rows * nb // 2

    own, near = near_pieces(panel, grid_cols)
    arrival = [[0], list(dict.fromkeys(rel for rel, _, _ in near))] + ([[2]] if grid_cols == 4 else [])
    order = [rel for rels in arrival for rel in rels]
    number = lambda pieces: [(order.index(rel) * nb + column // width, x) for rel, column, x in pieces]

    send, keep, store, plan = multiply_first(
        block_rows, block_cols, counts, arrival, panel, blocks[0, 0], nb, rows, grid_rows, grid_cols
    )
    phases = [own, near]
    if grid_cols == 4:
        far, send = lax.optimization_barrier((near[0][2], send))
        phases.append([(2, 0, lax.ppermute(far, "col", flips(4, 1)))])
    phases = [number(pieces) for pieces in phases]
    send = multiply_next(plan, 1, phases[1], store, rows, total=send)
    if grid_cols == 4:
        send = multiply_next(plan, 2, phases[2], store, rows, total=send)
    got = lax.ppermute(send, "row", flips(grid_rows, 1))
    rest = [piece for pieces in phases[1:] for piece in pieces]
    keep = multiply_next(plan, len(phases) + 1, rest, store, rows, total=keep)

    move = lambda x, i, stage: lax.ppermute(x, "row", flips(grid_rows, 1 << (bits - stage if i % 2 else stage)))
    if bits > 3:
        parts = add_and_split(keep, got, STREAMS)
        streams = [(parts[2 * i], move(parts[2 * i + 1], i, 1)) for i in range(STREAMS)]
        for stage in range(2, bits - 2):
            parts = [add_and_split(kept, x, 1) for kept, x in streams]
            streams = [(kept, move(x, i, stage)) for i, (kept, x) in enumerate(parts)]
        streams = [spread(kept, x, 1)[0] for kept, x in streams]
    else:
        streams = spread(keep, got, STREAMS)
    far = [move(stream[3], i, bits - 2) for i, stream in enumerate(streams)]
    near = [move(stream[2], i, bits - 2) for i, stream in enumerate(streams)]
    last = [move(relay(stream[1], x), i, bits - 1) for i, (stream, x) in enumerate(zip(streams, far))]
    streams = [(stream[0], x, y) for stream, x, y in zip(streams, near, last)]

    devices = grid_rows * grid_cols
    stacks, grams = gram_of(streams, devices)
    grams = lax.all_to_all(grams, ("row", "col"), 0, 0, tiled=True)
    return finish(grams, stacks, nb * width * devices)


def solution(mesh):
    in_specs = (
        P("row", "col", None, None, None),
        P("row", "col", None),
        P("row", "col", None),
        P("row", "col"),
        P(None, ("row", "col")),
    )
    out_specs = (P(None, ("row", "col")), P())
    return jax.shard_map(
        on_device, mesh=mesh, in_specs=in_specs, out_specs=out_specs, check_vma=False
    )
```
